32 devices in a mesh: pos: 4 (over y, core), mom: 8 (over z, x).
Axes of the slice: x: 2, y: 2, z: 4, core: 2. Of those that a mesh axis runs over, the one named last changes fastest.
Arguments:
- quasi_probability_grid: float32 [2, 512, 8192], P(None, 'pos', 'mom'), may hold values from 0 to 2
- potential_energy_map: float32 [2, 512], P(None, 'pos'), may hold values from -3 to 3
- contact_inflow_states: float32 [2, 2, 8192], P(None, None, 'mom'), may hold values from 0 to 2
- crystal_kelvin_field: float32 [512], P('pos'), may hold values from 0.6 to 1.6
- area_index_map: int32 [512], P('pos'), may hold values from 0 to 3
- damping_ratio_per_step: float32 [4], replicated, may hold values from 0.05 to 0.5
- equilibrium_populace: float32 [4], replicated, may hold values from 0.5 to 2
- conductance_per_step: float32 [4], replicated, may hold values from 0.05 to 0.45
Outputs:
- wigner_updated: float32 [2, 512, 8192], P(None, 'pos', 'mom')
- phonon_warmth_updated: float32 [512], P('pos')
The draws below stay inside these ranges and needn't reach their ends.
All inputs are finite; a program needn't handle non-finite values.
Results may differ from the reference program's by a relative error of at most 0.0003.
Values sent between devices are 32-bit elements; how exact they have to be, the bound alone decides.
A program may use at most 64 MiB of HBM per device.

```python
import math
import jax
import jax.numpy as jnp
from jax import lax

K = 8192
SUB = 2
AREA_KINDS = 4
SPOT_TOTAL = 128
CHANNEL_SPOTS = 512
STRIDE = 1
N_POS = 4


def set_ends(array, own_key, smallest, largest):
    place = [jax.random.randint(jax.random.fold_in(own_key, axis), (), 0, length) for axis, length in enumerate(array.shape)]
    longest = array.shape.index(max(array.shape))
    beside = place[:longest] + [(place[longest] + 1) % array.shape[longest]] + place[longest + 1:]
    return array.at[tuple(place)].set(smallest).at[tuple(beside)].set(largest)


def block_levels(own_key, shape, shards, low, top_value):
    loudness = 1.0
    for position, blocks in shards:
        steps = jax.random.uniform(jax.random.fold_in(jax.random.fold_in(own_key, 6), position), (blocks,), jnp.float32, low / len(shards), top_value / len(shards))
        loudness = loudness * jnp.repeat(jnp.exp(steps), shape[position] // blocks).reshape((-1,) + (1,) * (len(shape) - 1 - position))
    return loudness


def gaussian(stream_key, extent, spread, most, split=(), kind=jnp.bfloat16):
    array = jax.random.normal(stream_key, extent, jnp.float32) * spread
    if len(split) > 0:
        array = block_levels(stream_key, extent, split, -0.22, 0.18) * array
    return jnp.clip(array, min=-most, max=most).astype(kind)


def setup_inputs(seed: int = 0) -> dict:
    seeds = jax.random.split(jax.random.key(seed), 9)
    quasi_probability_grid = jnp.clip(2.0 * jax.random.uniform(seeds[0], (SUB, CHANNEL_SPOTS, K), jnp.float32) ** block_levels(seeds[0], (SUB, CHANNEL_SPOTS, K), ((1, 4), (2, 8)), -0.2, 0.2), 0.0, 2.0)
    potential_energy_map = gaussian(seeds[1], (SUB, CHANNEL_SPOTS), 0.5, 3.0, ((1, 4),), jnp.float32)
    contact_inflow_states = jnp.clip(2.0 * jax.random.uniform(seeds[2], (SUB, 2, K), jnp.float32) ** block_levels(seeds[2], (SUB, 2, K), ((2, 8),), -0.2, 0.2), 0.0, 2.0)
    crystal_kelvin_field = jnp.clip(0.6 + 1.0 * jax.random.uniform(seeds[3], (CHANNEL_SPOTS,), jnp.float32) ** block_levels(seeds[3], (CHANNEL_SPOTS,), ((0, 4),), -0.2, 0.2), 0.6, 1.6)
    area_index_map = set_ends(jax.random.randint(seeds[4], (CHANNEL_SPOTS,), 0, AREA_KINDS), jax.random.fold_in(seeds[4], 1), 0, AREA_KINDS - 1).astype(jnp.int32)
    damping_ratio_per_step = jnp.clip(jnp.exp(jax.random.uniform(seeds[5], (AREA_KINDS,), jnp.float32, math.log(0.05), math.log(0.5))), 0.05, 0.5)
    equilibrium_populace = jnp.clip(jnp.exp(jax.random.uniform(seeds[6], (AREA_KINDS,), jnp.float32, math.log(0.5), math.log(2.0))), 0.5, 2.0)
    conductance_per_step = jnp.clip(jax.random.uniform(seeds[7], (AREA_KINDS,), jnp.float32, 0.05, 0.45), 0.05, 0.45)
    return {"quasi_probability_grid": quasi_probability_grid, "potential_energy_map": potential_energy_map, "contact_inflow_states": contact_inflow_states, "crystal_kelvin_field": crystal_kelvin_field, "area_index_map": area_index_map, "damping_ratio_per_step": damping_ratio_per_step, "equilibrium_populace": equilibrium_populace, "conductance_per_step": conductance_per_step}


courant = 0.9
energy_top = 3.0
energy_shift = 0.25
band_offset = 0.5
potential_gain = 0.5
heat_gain = 0.5
heat_outflow = 0.1


def reference(quasi_probability_grid, potential_energy_map, contact_inflow_states, crystal_kelvin_field, area_index_map, damping_ratio_per_step, equilibrium_populace, conductance_per_step):
    mom_grid = jnp.arange(K, dtype=jnp.float32)
    unit_mom = (2.0 * mom_grid + 1.0) / K - 1.0
    velocity = courant * unit_mom
    band_minimum = energy_top * (unit_mom + energy_shift) ** 2
    indicator_matrix = (area_index_map[None, :] == jnp.arange(AREA_KINDS, dtype=jnp.int32)[:, None]).astype(jnp.float32)
    relax_rows = jnp.sum(indicator_matrix * damping_ratio_per_step[:, None], axis=0)
    populace_matrix = jnp.sum(indicator_matrix * equilibrium_populace[:, None], axis=0)
    coupling_slices = jnp.sum(indicator_matrix * conductance_per_step[:, None], axis=0)
    mode_minimum = band_offset * jnp.arange(SUB, dtype=jnp.float32)
    dist_index = jnp.arange(K, dtype=jnp.int32)
    signed = jnp.where(dist_index < K // 2, dist_index, dist_index - K)

    def one_block(block_index):
        front_slice = block_index * SPOT_TOTAL
        center = lax.dynamic_slice_in_dim(quasi_probability_grid, front_slice, SPOT_TOTAL, 1)
        prev_row = lax.dynamic_slice_in_dim(quasi_probability_grid, jnp.maximum(front_slice - 1, 0), 1, 1)
        next_row = lax.dynamic_slice_in_dim(quasi_probability_grid, jnp.minimum(front_slice + SPOT_TOTAL, CHANNEL_SPOTS - 1), 1, 1)
        prev_row = jnp.where(block_index == 0, contact_inflow_states[:, 0:1, :], prev_row)
        next_row = jnp.where(block_index == N_POS - 1, contact_inflow_states[:, 1:2, :], next_row)
        below_rows = jnp.concatenate([prev_row, center[:, :-1, :]], axis=1)
        above_rows = jnp.concatenate([center[:, 1:, :], next_row], axis=1)
        drift_term = jnp.where(velocity > 0, -velocity * (center - below_rows), -velocity * (above_rows - center))
        warmth_piece = lax.dynamic_slice_in_dim(crystal_kelvin_field, front_slice, SPOT_TOTAL, 0)
        dens_block = lax.dynamic_slice_in_dim(populace_matrix, front_slice, SPOT_TOTAL, 0)
        relax_block = lax.dynamic_slice_in_dim(relax_rows, front_slice, SPOT_TOTAL, 0)
        equilibrium = dens_block[None, :, None] * jnp.exp(
            -(band_minimum[None, None, :] + mode_minimum[:, None, None]) / warmth_piece[None, :, None])
        places = front_slice + jnp.arange(SPOT_TOTAL, dtype=jnp.int32)
        ahead_index = jnp.clip(places[:, None] + STRIDE * signed[None, :], 0, CHANNEL_SPOTS - 1).astype(jnp.int32)
        behind_index = jnp.clip(places[:, None] - STRIDE * signed[None, :], 0, CHANNEL_SPOTS - 1).astype(jnp.int32)
        pot_diff = jnp.take(potential_energy_map, ahead_index, axis=1) - jnp.take(potential_energy_map, behind_index, axis=1)
        spectrum = jnp.fft.ifft(center, axis=-1) * K
        nonlocal_part = (potential_gain / K) * jnp.imag(jnp.fft.fft(pot_diff * spectrum, axis=-1))
        updated = center + drift_term + nonlocal_part - relax_block[None, :, None] * (center - equilibrium)
        joule_input = (heat_gain / K) * relax_block * jnp.sum(band_minimum[None, None, :] * (center - equilibrium), axis=(0, 2))
        return updated, joule_input

    new_blocks, heat_blocks = lax.map(one_block, jnp.arange(N_POS, dtype=jnp.int32))
    wigner_updated = jnp.transpose(new_blocks, (1, 0, 2, 3)).reshape(SUB, CHANNEL_SPOTS, K)
    joule_input = heat_blocks.reshape(CHANNEL_SPOTS)
    ones_margin = jnp.ones((1,), jnp.float32)
    warmth_padded_vector = jnp.concatenate([ones_margin, crystal_kelvin_field, ones_margin])
    phonon_warmth_updated = (crystal_kelvin_field + coupling_slices * (warmth_padded_vector[2:] - 2.0 * crystal_kelvin_field + warmth_padded_vector[:-2])
                        + joule_input - heat_outflow * (crystal_kelvin_field - 1.0))
    return wigner_updated, phonon_warmth_updated
```

```python
import functools

import jax
import jax.numpy as jnp
import numpy as np
from jax import lax
from jax.experimental import pallas as pl
from jax.experimental.pallas import tpu as pltpu
from jax.sharding import PartitionSpec as P

K = 8192
LANES = 128
FOLD = K // LANES
HALF = FOLD // 2

courant = 0.9
energy_top = 3.0
energy_shift = 0.25
band_offset = 0.5
potential_gain = 0.5
heat_gain = 0.5
heat_outflow = 0.1

F32 = jnp.float32
BF16 = jnp.bfloat16
MESH = pl.DeviceIdType.MESH


def unit_root(step, length):
    angle = 2.0 * np.pi * step / length
    return float(np.cos(angle)), float(np.sin(angle))


def turned(re, im, c, s):
    if s == 0.0 and c == 1.0:
        return re, im
    if im is None:
        return re * c, re * s
    if abs(c) < 1e-12:
        return -im * s, re * s
    return re * c - im * s, re * s + im * c


def plus(a, b):
    if a is None:
        return b
    if b is None:
        return a
    return a + b


def minus(a, b):
    if b is None:
        return a
    if a is None:
        return -b
    return a - b


def real_forward(xs):
    n = len(xs)
    if n == 2:
        return [(xs[0] + xs[1], None), (xs[0] - xs[1], None)]
    even, odd = real_forward(xs[0::2]), real_forward(xs[1::2])
    out = [None] * (n // 2 + 1)
    for k in range(n // 4 + 1):
        c, s = unit_root(k, n)
        orr, oi = turned(odd[k][0], odd[k][1], c, s)
        er, ei = even[k]
        if 4 * k == n:
            out[k] = (er, odd[k][0])
            continue
        out[k] = (er + orr, plus(ei, oi))
        low = minus(oi, ei)
        out[n // 2 - k] = (er - orr, low)
    return out


def real_inverse(spec):
    n = 2 * (len(spec) - 1)
    if n == 2:
        a, b = spec[0][0], spec[1][0]
        return [a + b, a - b]
    even, odd = [], []
    for k in range(n // 4 + 1):
        ar, ai = spec[k]
        br, bi = spec[n // 2 - k]
        c, s = unit_root(k, n)
        if 4 * k == n:
            even.append((ar + ar, None))
            odd.append((-(ai + ai), None))
            continue
        if k == 0:
            even.append((ar + br, None))
            odd.append((ar - br, None))
            continue
        even.append((ar + br, minus(ai, bi)))
        odd.append(turned(ar - br, plus(ai, bi), c, s))
    xe, xo = real_inverse(even), real_inverse(odd)
    out = [None] * n
    out[0::2], out[1::2] = xe, xo
    return out


def fill_tables(weight_ref, twist_ref):
    row = lax.broadcasted_iota(jnp.int32, (LANES, LANES), 0)
    lane = lax.broadcasted_iota(jnp.int32, (LANES, LANES), 1)
    angle = lax.rem(row * lane, LANES).astype(F32) * (2.0 * np.pi / LANES)
    c, s = jnp.cos(angle), jnp.sin(angle)
    for n, blocks in enumerate((((c, s), (-s, c)), ((c, -s), (s, c)))):
        for a in range(2):
            for b in range(2):
                at = (pl.ds(a * LANES, LANES), pl.ds(b * LANES, LANES))
                high = blocks[a][b].astype(BF16)
                weight_ref[(2 * n,) + at] = high
                weight_ref[(2 * n + 1,) + at] = (blocks[a][b] - high.astype(F32)).astype(BF16)
    count = twist_ref.shape[1]
    angle = (row * lane)[:count].astype(F32) * (2.0 * np.pi / K)
    twist_ref[0] = jnp.cos(angle)
    twist_ref[1] = jnp.sin(angle)


def split_dot(a, high, low):
    a_high = a.astype(BF16)
    a_low = (a - a_high.astype(F32)).astype(BF16)
    dot = functools.partial(jnp.dot, preferred_element_type=F32)
    return dot(a_high, high) + (dot(a_low, high) + dot(a_high, low))


def kernel(
    sizes,
    grid_hbm,
    pot_hbm,
    contact_hbm,
    warmth_hbm,
    area_hbm,
    damping_hbm,
    populace_hbm,
    conduct_hbm,
    out_ref,
    warm_ref,
    grid_ref,
    pot_ref,
    contact_ref,
    warmth_ref,
    area_ref,
    damping_ref,
    populace_ref,
    conduct_ref,
    weight_ref,
    twist_ref,
    recv,
    back_send,
    back_recv,
    halo_low,
    halo_high,
    pot_all,
    warmth_all,
    heat_send,
    heat_all,
    pot_table,
    work,
    fwd_send_sem,
    fwd_recv_sem,
    ret_send_sem,
    ret_recv_sem,
    halo_send_sem,
    halo_recv_sem,
    small_send_sem,
    small_recv_sem,
    heat_sem,
    load_sem,
    mom_ready,
    pos_ready,
):
    bands, rows, cols, n_pos, n_mom = sizes
    share = rows // n_mom
    pieces = cols // LANES
    grid_len = n_pos * rows
    pos = lax.axis_index("pos")
    me = lax.axis_index("mom")

    level_size = inner_size(n_mom)
    my_level, my_place = me // level_size, lax.rem(me, level_size)

    def pos_peer(d):
        return lax.rem(pos + d, n_pos)

    def over_peers(do):
        for d in range(1, n_mom):
            do(lax.rem(me + d, n_mom))

    def wait_all(ref, count, sem):
        block = ref.at[pl.ds(0, count)]
        pltpu.make_async_copy(block, block, sem).wait()

    small = (
        (pot_hbm, pot_ref),
        (contact_hbm, contact_ref),
        (warmth_hbm, warmth_ref),
        (area_hbm, area_ref),
        (damping_hbm, damping_ref),
        (populace_hbm, populace_ref),
        (conduct_hbm, conduct_ref),
    )
    loads = [
        pltpu.make_async_copy(src, dst, load_sem.at[n])
        for n, (src, dst) in enumerate(((grid_hbm, grid_ref),) + small)
    ]

    def small_copy(d, which):
        return pltpu.make_async_remote_copy(
            src_ref=warmth_hbm if which else pot_hbm,
            dst_ref=(warmth_all if which else pot_all).at[pos],
            send_sem=small_send_sem.at[which],
            recv_sem=small_recv_sem.at[which],
            device_id=(pos_peer(d), me),
            device_id_type=MESH,
        )

    def halo_copy(up):
        return pltpu.make_async_remote_copy(
            src_ref=grid_hbm.at[:, pl.ds(rows - 8, 8) if up else pl.ds(0, 8), :],
            dst_ref=halo_low if up else halo_high,
            send_sem=halo_send_sem.at[0 if up else 1],
            recv_sem=halo_recv_sem.at[0 if up else 1],
            device_id=(pos_peer(1 if up else n_pos - 1), me),
            device_id_type=MESH,
        )

    def forward_copy(band, peer):
        return pltpu.make_async_remote_copy(
            src_ref=grid_hbm.at[band, pl.ds(pl.multiple_of(peer * share, share), share), :],
            dst_ref=recv.at[band, me],
            send_sem=fwd_send_sem.at[band],
            recv_sem=fwd_recv_sem.at[band],
            device_id=(pos, peer),
            device_id_type=MESH,
        )

    def return_copy(band, peer):
        return pltpu.make_async_remote_copy(
            src_ref=back_send.at[band, peer],
            dst_ref=back_recv.at[band, me],
            send_sem=ret_send_sem.at[band],
            recv_sem=ret_recv_sem.at[band],
            device_id=(pos, peer),
            device_id_type=MESH,
        )

    def heat_copy(peer):
        return pltpu.make_async_remote_copy(
            src_ref=heat_send,
            dst_ref=heat_all.at[me],
            send_sem=heat_sem.at[0],
            recv_sem=heat_sem.at[1],
            device_id=(pos, peer),
            device_id_type=MESH,
        )

    def start_forward(band, peer):
        forward_copy(band, peer).start()

    for load in loads:
        load.start()

    barrier = pltpu.get_barrier_semaphore()
    for peer in range(1, n_mom):

        @pl.when(me < peer)
        def _(peer=peer):
            pl.semaphore_signal(barrier, inc=1, device_id=(pos, peer), device_id_type=MESH)

    for peer in range(1, n_pos):

        @pl.when(pos < peer)
        def _(peer=peer):
            pl.semaphore_signal(barrier, inc=1, device_id=(peer, me), device_id_type=MESH)

    @pl.when(me + pos > 0)
    def _():
        pl.semaphore_wait(barrier, me + pos)

    for peer in range(n_mom - 1):

        @pl.when(peer < me)
        def _(peer=peer):
            pl.semaphore_signal(
                mom_ready.at[my_level], inc=1, device_id=(pos, peer), device_id_type=MESH
            )

    for peer in range(n_pos - 1):

        @pl.when(peer < pos)
        def _(peer=peer):
            pl.semaphore_signal(pos_ready, inc=1, device_id=(peer, me), device_id_type=MESH)

    for peer in range(n_mom - 1):
        pl.when(peer < me)(functools.partial(start_forward, 0, peer))

    fill_tables(weight_ref, twist_ref)

    for level in range(n_mom // level_size):
        others = jnp.where(level == my_level, level_size - 1 - my_place, level_size)

        @pl.when((level >= my_level) & (others > 0))
        def _(level=level, others=others):
            pl.semaphore_wait(mom_ready.at[level], others)

        for peer in range(max(level * level_size, 1), (level + 1) * level_size):
            pl.when(peer > me)(functools.partial(start_forward, 0, peer))

    @pl.when(pos < n_pos - 1)
    def _():
        pl.semaphore_wait(pos_ready, n_pos - 1 - pos)

    for d in range(1, n_pos):
        small_copy(d, 0).start()
        small_copy(d, 1).start()

    @pl.when(pos < n_pos - 1)
    def _():
        halo_copy(True).start()

    @pl.when(pos > 0)
    def _():
        halo_copy(False).start()

    for band in range(1, bands):
        over_peers(functools.partial(start_forward, band))
    for load in loads:
        load.wait()

    own = pl.ds(pl.multiple_of(me * share, share), share)
    for band in range(bands):
        recv[band, me] = grid_ref[band, own, :]
    pot_all[pos] = pot_ref[...]
    warmth_all[pos] = warmth_ref[...]

    @pl.when(pos == 0)
    def _():
        halo_low[:, 7:8, :] = contact_ref[:, 0:1, :]

    @pl.when(pos > 0)
    def _():
        halo_copy(True).wait_recv()

    @pl.when(pos == n_pos - 1)
    def _():
        halo_high[:, 0:1, :] = contact_ref[:, 1:2, :]

    @pl.when(pos < n_pos - 1)
    def _():
        halo_copy(False).wait_recv()

    def picked(values):
        total = jnp.zeros((1, rows), F32)
        for n in range(values.shape[1]):
            total = jnp.where(area_ref[...] == n, values[0:1, n : n + 1], total)
        return total

    def column(row):
        return jnp.transpose(jnp.broadcast_to(row, (rows, rows)))

    warmth = warmth_ref[...]
    relax = picked(damping_ref)
    conduct = picked(conduct_ref)
    warmth_col = column(warmth)
    relax_col = column(relax)
    dens_col = column(picked(populace_ref))
    cold_col = -1.0 / warmth_col
    row_iota = lax.broadcasted_iota(jnp.int32, (rows, LANES), 0)

    def local_piece(c, heat):
        lane = pl.ds(pl.multiple_of(c * LANES, LANES), LANES)
        mom = lax.broadcasted_iota(jnp.int32, (1, LANES), 1) + (me * cols + c * LANES)
        unit = (2.0 * mom.astype(F32) + 1.0) / K - 1.0
        velocity = courant * unit
        energy = energy_top * (unit + energy_shift) ** 2
        for band in range(bands):
            f = grid_ref[band, :, lane]
            below = jnp.where(row_iota == 0, halo_low[band, 7:8, lane], pltpu.roll(f, 1, 0))
            above = jnp.where(
                row_iota == rows - 1, halo_high[band, 0:1, lane], pltpu.roll(f, rows - 1, 0)
            )
            drift = -velocity * jnp.where(velocity > 0, f - below, above - f)
            excess = f - dens_col * jnp.exp((energy + band_offset * band) * cold_col)
            out_ref[band, :, lane] = f + drift - relax_col * excess
            heat = heat + energy * excess
        return heat

    heat = lax.fori_loop(0, pieces, local_piece, jnp.zeros((rows, LANES), F32))
    heat_row = jnp.sum(jnp.transpose(heat), axis=0, keepdims=True)
    heat_send[...] = jnp.broadcast_to(heat_row, (8, rows))
    heat_all[me] = jnp.broadcast_to(heat_row, (8, rows))
    over_peers(lambda peer: heat_copy(peer).start())

    wait_all(pot_all, n_pos - 1, small_recv_sem.at[0])
    wait_all(warmth_all, n_pos - 1, small_recv_sem.at[1])
    n_step = grid_len // FOLD
    base = pos * rows + me * share - HALF
    turn = lax.rem(2 * grid_len - base, grid_len)
    step_iota = lax.broadcasted_iota(jnp.int32, (n_step, grid_len), 0)
    place_iota = lax.broadcasted_iota(jnp.int32, (LANES, LANES), 0)
    lane_iota = lax.broadcasted_iota(jnp.int32, (LANES, LANES), 1)
    signed = jnp.where(lane_iota < LANES // 2, lane_iota, lane_iota - LANES) * FOLD
    for band in range(bands):
        profile = jnp.concatenate(
            [pot_all[j, band : band + 1, :] for j in range(n_pos)], axis=1
        )
        first = profile[:, 0:1]
        last = profile[:, grid_len - 1 : grid_len]
        profile = jnp.broadcast_to(profile, (n_step, grid_len))
        for side in range(2):
            stack = profile
            for m in range(1, n_step):
                shift = (grid_len - FOLD * m) % grid_len if side == 0 else FOLD * m
                stack = jnp.where(step_iota == m, pltpu.roll(profile, shift, 1), stack)
            stack = pltpu.roll(stack, turn, 1)[:, :LANES]
            stack = jnp.transpose(jnp.concatenate([stack] * (LANES // n_step), axis=0))
            index = base + place_iota + (signed if side == 0 else -signed)
            stack = jnp.where(index < 0, first, jnp.where(index > grid_len - 1, last, stack))
            pot_table[band, side] = stack

    scale = potential_gain / K

    def forward_wait(band):
        wait_all(recv.at[band], n_mom - 1, fwd_recv_sem.at[band])

    def transform(band):
        cells = [
            recv[band, j, :, c * LANES : (c + 1) * LANES]
            for j in range(n_mom)
            for c in range(pieces)
        ]
        spec = real_forward(cells)
        for s, (re, im) in enumerate(spec):
            at = pl.ds(s * share, share)
            c_row, s_row = twist_ref[0, s : s + 1, :], twist_ref[1, s : s + 1, :]
            if im is None:
                work[at, :LANES] = re * c_row
                work[at, LANES:] = re * s_row
            else:
                work[at, :LANES] = re * c_row - im * s_row
                work[at, LANES:] = re * s_row + im * c_row
        work[...] = split_dot(work[...], weight_ref[0], weight_ref[1])
        for s in range(HALF + 1):
            at = pl.ds(s * share, share)
            differ = (
                pot_table[band, 0, HALF + s : HALF + s + share, :]
                - pot_table[band, 1, HALF - s : HALF - s + share, :]
            ) * scale
            work[at, :LANES] = work[at, :LANES] * differ
            work[at, LANES:] = work[at, LANES:] * differ
        work[...] = split_dot(work[...], weight_ref[2], weight_ref[3])
        spec = []
        for s in range(HALF + 1):
            at = pl.ds(s * share, share)
            c_row, s_row = twist_ref[0, s : s + 1, :], twist_ref[1, s : s + 1, :]
            re, im = work[at, :LANES], work[at, LANES:]
            spec.append((im * c_row - re * s_row, re * c_row + im * s_row))
        cells = real_inverse(spec)
        for j in range(n_mom):
            for c in range(pieces):
                back_send[band, j, :, c * LANES : (c + 1) * LANES] = cells[j * pieces + c]
        back_recv[band, me] = back_send[band, me]

    def return_start(band):
        over_peers(lambda peer: return_copy(band, peer).start())

    def one_band(band, carry):
        forward_wait(band)

        transform(band)
        return_start(band)
        return carry

    lax.fori_loop(0, bands, one_band, 0)

    def add_back(band, carry):
        wait_all(back_recv.at[band], n_mom - 1, ret_recv_sem.at[band])
        for j in range(n_mom):
            at = pl.ds(j * share, share)
            out_ref[band, at, :] = out_ref[band, at, :] + back_recv[band, j]
        return carry

    lax.fori_loop(0, bands - 1, add_back, 0)

    wait_all(heat_all, n_mom - 1, heat_sem.at[1])
    total = heat_all[0, 0:1, :]
    for j in range(1, n_mom):
        total = total + heat_all[j, 0:1, :]
    lane_row = lax.broadcasted_iota(jnp.int32, (1, rows), 1)
    low_edge = warmth_all[jnp.maximum(pos - 1, 0), 0:1, rows - 1 : rows]
    high_edge = warmth_all[jnp.minimum(pos + 1, n_pos - 1), 0:1, 0:1]
    low_edge = jnp.where(pos == 0, jnp.ones_like(low_edge), low_edge)
    high_edge = jnp.where(pos == n_pos - 1, jnp.ones_like(high_edge), high_edge)
    before = jnp.where(lane_row == 0, low_edge, pltpu.roll(warmth, 1, 1))
    after = jnp.where(lane_row == rows - 1, high_edge, pltpu.roll(warmth, rows - 1, 1))
    warm_ref[...] = (
        warmth
        + conduct * (after - 2.0 * warmth + before)
        + heat_gain / K * relax * total
        - heat_outflow * (warmth - 1.0)
    )

    wait_all(pot_all, n_pos - 1, small_send_sem.at[0])
    wait_all(warmth_all, n_pos - 1, small_send_sem.at[1])

    @pl.when(pos < n_pos - 1)
    def _():
        halo_copy(True).wait_send()

    @pl.when(pos > 0)
    def _():
        halo_copy(False).wait_send()

    wait_all(heat_all, n_mom - 1, heat_sem.at[0])
    for band in range(bands):
        wait_all(recv.at[band], n_mom - 1, fwd_send_sem.at[band])
        if band < bands - 1:
            wait_all(back_send.at[band], n_mom - 1, ret_send_sem.at[band])
    add_back(bands - 1, 0)
    wait_all(back_send.at[bands - 1], n_mom - 1, ret_send_sem.at[bands - 1])


def write_out(grid_ref, warm_ref, grid_hbm, warm_hbm, sem):
    bands = grid_ref.shape[0]
    copies = [
        pltpu.make_async_copy(grid_ref.at[band], grid_hbm.at[band], sem.at[band])
        for band in range(bands)
    ]
    copies.append(pltpu.make_async_copy(warm_ref, warm_hbm, sem.at[bands]))
    for copy in copies:
        copy.start()
    for copy in copies:
        copy.wait()


def inner_size(n):
    inner = 1
    while inner * inner * 4 <= n:
        inner *= 2
    return inner if n % inner == 0 else 1


def body(
    quasi_probability_grid,
    potential_energy_map,
    contact_inflow_states,
    crystal_kelvin_field,
    area_index_map,
    damping_ratio_per_step,
    equilibrium_populace,
    conductance_per_step,
):
    bands, rows, cols = quasi_probability_grid.shape
    n_pos = lax.axis_size("pos")
    n_mom = lax.axis_size("mom")
    share = rows // n_mom
    kinds = damping_ratio_per_step.shape[0]
    vmem = pl.BlockSpec(memory_space=pltpu.VMEM)
    hbm = pl.BlockSpec(memory_space=pltpu.HBM)
    dma = pltpu.SemaphoreType.DMA
    regular = pltpu.SemaphoreType.REGULAR
    shapes = (
        jax.ShapeDtypeStruct((bands, rows, cols), F32),
        jax.ShapeDtypeStruct((1, rows), F32),
    )
    updated, warm = pl.pallas_call(
        functools.partial(kernel, (bands, rows, cols, n_pos, n_mom)),
        out_shape=shapes,
        in_specs=[hbm] * 8,
        out_specs=(vmem, vmem),
        scratch_shapes=[
            pltpu.VMEM((bands, rows, cols), F32),
            pltpu.VMEM((bands, rows), F32),
            pltpu.VMEM((bands, 2, cols), F32),
            pltpu.VMEM((1, rows), F32),
            pltpu.VMEM((1, rows), jnp.int32),
            pltpu.VMEM((1, kinds), F32),
            pltpu.VMEM((1, kinds), F32),
            pltpu.VMEM((1, kinds), F32),
            pltpu.VMEM((4, 2 * LANES, 2 * LANES), BF16),
            pltpu.VMEM((2, HALF + 8, LANES), F32),
            pltpu.VMEM((bands, n_mom, share, cols), F32),
            pltpu.VMEM((bands, n_mom, share, cols), F32),
            pltpu.VMEM((bands, n_mom, share, cols), F32),
            pltpu.VMEM((bands, 8, cols), F32),
            pltpu.VMEM((bands, 8, cols), F32),
            pltpu.VMEM((n_pos, bands, rows), F32),
            pltpu.VMEM((n_pos, 1, rows), F32),
            pltpu.VMEM((8, rows), F32),
            pltpu.VMEM((n_mom, 8, rows), F32),
            pltpu.VMEM((bands, 2, LANES, LANES), F32),
            pltpu.VMEM(((HALF + 1) * share, 2 * LANES), F32),
            dma((bands,)),
            dma((bands,)),
            dma((bands,)),
            dma((bands,)),
            dma((2,)),
            dma((2,)),
            dma((2,)),
            dma((2,)),
            dma((2,)),
            dma((8,)),
            regular((n_mom // inner_size(n_mom),)),
            regular,
        ],
        compiler_params=pltpu.CompilerParams(
            collective_id=0, has_side_effects=True, vmem_limit_bytes=52 * 1024 * 1024
        ),
    )(
        *(
            pltpu.with_memory_space_constraint(operand, pltpu.HBM)
            for operand in (
                quasi_probability_grid,
                potential_energy_map,
                contact_inflow_states,
                crystal_kelvin_field[None],
                area_index_map[None],
                damping_ratio_per_step[None],
                equilibrium_populace[None],
                conductance_per_step[None],
            )
        )
    )
    updated, warm = pl.pallas_call(
        write_out,
        out_shape=shapes,
        in_specs=[vmem, vmem],
        out_specs=(hbm, hbm),
        scratch_shapes=[dma((bands + 1,))],
        compiler_params=pltpu.CompilerParams(vmem_limit_bytes=8 * 1024 * 1024),
    )(updated, warm)
    return updated, warm[0]


def solution(mesh):
    return jax.shard_map(
        body,
        mesh=mesh,
        in_specs=(
            P(None, "pos", "mom"),
            P(None, "pos"),
            P(None, None, "mom"),
            P("pos"),
            P("pos"),
            P(),
            P(),
            P(),
        ),
        out_specs=(P(None, "pos", "mom"), P("pos")),
        check_vma=False,
    )
```

```python
import functools

import jax
import jax.numpy as jnp
import numpy as np
from jax import lax
from jax.experimental import pallas as pl
from jax.experimental.pallas import tpu as pltpu
from jax.sharding import PartitionSpec as P

K = 8192
LANES = 128
FOLD = K // LANES
HALF = FOLD // 2

courant = 0.9
energy_top = 3.0
energy_shift = 0.25
band_offset = 0.5
potential_gain = 0.5
heat_gain = 0.5
heat_outflow = 0.1

F32 = jnp.float32
BF16 = jnp.bfloat16
MESH = pl.DeviceIdType.MESH


def unit_root(step, length):
    angle = 2.0 * np.pi * step / length
    return float(np.cos(angle)), float(np.sin(angle))


def turned(re, im, c, s):
    if s == 0.0 and c == 1.0:
        return re, im
    if im is None:
        return re * c, re * s
    if abs(c) < 1e-12:
        return -im * s, re * s
    return re * c - im * s, re * s + im * c


def plus(a, b):
    if a is None:
        return b
    if b is None:
        return a
    return a + b


def minus(a, b):
    if b is None:
        return a
    if a is None:
        return -b
    return a - b


def real_forward(xs):
    n = len(xs)
    if n == 2:
        return [(xs[0] + xs[1], None), (xs[0] - xs[1], None)]
    even, odd = real_forward(xs[0::2]), real_forward(xs[1::2])
    out = [None] * (n // 2 + 1)
    for k in range(n // 4 + 1):
        c, s = unit_root(k, n)
        orr, oi = turned(odd[k][0], odd[k][1], c, s)
        er, ei = even[k]
        if 4 * k == n:
            out[k] = (er, odd[k][0])
            continue
        out[k] = (er + orr, plus(ei, oi))
        low = minus(oi, ei)
        out[n // 2 - k] = (er - orr, low)
    return out


def real_inverse(spec):
    n = 2 * (len(spec) - 1)
    if n == 2:
        a, b = spec[0][0], spec[1][0]
        return [a + b, a - b]
    even, odd = [], []
    for k in range(n // 4 + 1):
        ar, ai = spec[k]
        br, bi = spec[n // 2 - k]
        c, s = unit_root(k, n)
        if 4 * k == n:
            even.append((ar + ar, None))
            odd.append((-(ai + ai), None))
            continue
        if k == 0:
            even.append((ar + br, None))
            odd.append((ar - br, None))
            continue
        even.append((ar + br, minus(ai, bi)))
        odd.append(turned(ar - br, plus(ai, bi), c, s))
    xe, xo = real_inverse(even), real_inverse(odd)
    out = [None] * n
    out[0::2], out[1::2] = xe, xo
    return out


def fill_tables(weight_ref, twist_ref):
    row = lax.broadcasted_iota(jnp.int32, (LANES, LANES), 0)
    lane = lax.broadcasted_iota(jnp.int32, (LANES, LANES), 1)
    angle = lax.rem(row * lane, LANES).astype(F32) * (2.0 * np.pi / LANES)
    c, s = jnp.cos(angle), jnp.sin(angle)
    for n, blocks in enumerate((((c, s), (-s, c)), ((c, -s), (s, c)))):
        for a in range(2):
            for b in range(2):
                at = (pl.ds(a * LANES, LANES), pl.ds(b * LANES, LANES))
                high = blocks[a][b].astype(BF16)
                weight_ref[(2 * n,) + at] = high
                weight_ref[(2 * n + 1,) + at] = (blocks[a][b] - high.astype(F32)).astype(BF16)
    count = twist_ref.shape[1]
    angle = (row * lane)[:count].astype(F32) * (2.0 * np.pi / K)
    twist_ref[0] = jnp.cos(angle)
    twist_ref[1] = jnp.sin(angle)


def split_dot(a, high, low):
    a_high = a.astype(BF16)
    a_low = (a - a_high.astype(F32)).astype(BF16)
    dot = functools.partial(jnp.dot, preferred_element_type=F32)
    return dot(a_high, high) + (dot(a_low, high) + dot(a_high, low))


def kernel(
    sizes,
    grid_hbm,
    pot_hbm,
    contact_hbm,
    warmth_hbm,
    area_hbm,
    damping_hbm,
    populace_hbm,
    conduct_hbm,
    out_ref,
    warm_ref,
    grid_ref,
    pot_ref,
    contact_ref,
    warmth_ref,
    area_ref,
    damping_ref,
    populace_ref,
    conduct_ref,
    weight_ref,
    twist_ref,
    recv,
    back_send,
    back_recv,
    halo_low,
    halo_high,
    pot_all,
    warmth_all,
    heat_send,
    heat_all,
    pot_table,
    work,
    fwd_send_sem,
    fwd_recv_sem,
    ret_send_sem,
    ret_recv_sem,
    halo_send_sem,
    halo_recv_sem,
    small_send_sem,
    small_recv_sem,
    heat_sem,
    load_sem,
    mom_ready,
    pos_ready,
):
    bands, rows, cols, n_pos, n_mom = sizes
    share = rows // n_mom
    pieces = cols // LANES
    grid_len = n_pos * rows
    pos = lax.axis_index("pos")
    me = lax.axis_index("mom")

    level_size = inner_size(n_mom)
    my_level, my_place = me // level_size, lax.rem(me, level_size)

    def pos_peer(d):
        return lax.rem(pos + d, n_pos)

    def over_peers(do):
        for d in range(1, n_mom):
            do(lax.rem(me + d, n_mom))

    def wait_all(ref, count, sem):
        block = ref.at[pl.ds(0, count)]
        pltpu.make_async_copy(block, block, sem).wait()

    small = (
        (pot_hbm, pot_ref),
        (contact_hbm, contact_ref),
        (warmth_hbm, warmth_ref),
        (area_hbm, area_ref),
        (damping_hbm, damping_ref),
        (populace_hbm, populace_ref),
        (conduct_hbm, conduct_ref),
    )
    loads = [
        pltpu.make_async_copy(src, dst, load_sem.at[n])
        for n, (src, dst) in enumerate(((grid_hbm, grid_ref),) + small)
    ]

    def small_copy(d, which):
        return pltpu.make_async_remote_copy(
            src_ref=warmth_hbm if which else pot_hbm,
            dst_ref=(warmth_all if which else pot_all).at[pos],
            send_sem=small_send_sem.at[which],
            recv_sem=small_recv_sem.at[which],
            device_id=(pos_peer(d), me),
            device_id_type=MESH,
        )

    def halo_copy(up):
        return pltpu.make_async_remote_copy(
            src_ref=grid_hbm.at[:, pl.ds(rows - 8, 8) if up else pl.ds(0, 8), :],
            dst_ref=halo_low if up else halo_high,
            send_sem=halo_send_sem.at[0 if up else 1],
            recv_sem=halo_recv_sem.at[0 if up else 1],
            device_id=(pos_peer(1 if up else n_pos - 1), me),
            device_id_type=MESH,
        )

    def forward_copy(band, peer):
        return pltpu.make_async_remote_copy(
            src_ref=grid_hbm.at[band, pl.ds(pl.multiple_of(peer * share, share), share), :],
            dst_ref=recv.at[band, me],
            send_sem=fwd_send_sem.at[band],
            recv_sem=fwd_recv_sem.at[band],
            device_id=(pos, peer),
            device_id_type=MESH,
        )

    def return_copy(band, peer):
        return pltpu.make_async_remote_copy(
            src_ref=back_send.at[band, peer],
            dst_ref=back_recv.at[band, me],
            send_sem=ret_send_sem.at[band],
            recv_sem=ret_recv_sem.at[band],
            device_id=(pos, peer),
            device_id_type=MESH,
        )

    def heat_copy(peer):
        return pltpu.make_async_remote_copy(
            src_ref=heat_send,
            dst_ref=heat_all.at[me],
            send_sem=heat_sem.at[0],
            recv_sem=heat_sem.at[1],
            device_id=(pos, peer),
            device_id_type=MESH,
        )

    def start_forward(band, peer):
        forward_copy(band, peer).start()

    for load in loads:
        load.start()

    barrier = pltpu.get_barrier_semaphore()
    for peer in range(1, n_mom):

        @pl.when(me < peer)
        def _(peer=peer):
            pl.semaphore_signal(barrier, inc=1, device_id=(pos, peer), device_id_type=MESH)

    for peer in range(1, n_pos):

        @pl.when(pos < peer)
        def _(peer=peer):
            pl.semaphore_signal(barrier, inc=1, device_id=(peer, me), device_id_type=MESH)

    @pl.when(me + pos > 0)
    def _():
        pl.semaphore_wait(barrier, me + pos)

    for peer in range(n_mom - 1):

        @pl.when(peer < me)
        def _(peer=peer):
            pl.semaphore_signal(
                mom_ready.at[my_level], inc=1, device_id=(pos, peer), device_id_type=MESH
            )

    for peer in range(n_pos - 1):

        @pl.when(peer < pos)
        def _(peer=peer):
            pl.semaphore_signal(pos_ready, inc=1, device_id=(peer, me), device_id_type=MESH)

    for peer in range(n_mom - 1):
        pl.when(peer < me)(functools.partial(start_forward, 0, peer))

    fill_tables(weight_ref, twist_ref)

    for level in range(n_mom // level_size):
        others = jnp.where(level == my_level, level_size - 1 - my_place, level_size)

        @pl.when((level >= my_level) & (others > 0))
        def _(level=level, others=others):
            pl.semaphore_wait(mom_ready.at[level], others)

        for peer in range(max(level * level_size, 1), (level + 1) * level_size):
            pl.when(peer > me)(functools.partial(start_forward, 0, peer))

    @pl.when(pos < n_pos - 1)
    def _():
        pl.semaphore_wait(pos_ready, n_pos - 1 - pos)

    for d in range(1, n_pos):
        small_copy(d, 0).start()
        small_copy(d, 1).start()

    @pl.when(pos < n_pos - 1)
    def _():
        halo_copy(True).start()

    @pl.when(pos > 0)
    def _():
        halo_copy(False).start()

    for band in range(1, bands):
        over_peers(functools.partial(start_forward, band))
    for load in loads:
        load.wait()

    own = pl.ds(pl.multiple_of(me * share, share), share)
    for band in range(bands):
        recv[band, me] = grid_ref[band, own, :]
    pot_all[pos] = pot_ref[...]
    warmth_all[pos] = warmth_ref[...]

    @pl.when(pos == 0)
    def _():
        halo_low[:, 7:8, :] = contact_ref[:, 0:1, :]

    @pl.when(pos > 0)
    def _():
        halo_copy(True).wait_recv()

    @pl.when(pos == n_pos - 1)
    def _():
        halo_high[:, 0:1, :] = contact_ref[:, 1:2, :]

    @pl.when(pos < n_pos - 1)
    def _():
        halo_copy(False).wait_recv()

    def picked(values):
        total = jnp.zeros((1, rows), F32)
        for n in range(values.shape[1]):
            total = jnp.where(area_ref[...] == n, values[0:1, n : n + 1], total)
        return total

    def column(row):
        return jnp.transpose(jnp.broadcast_to(row, (rows, rows)))

    warmth = warmth_ref[...]
    relax = picked(damping_ref)
    conduct = picked(conduct_ref)
    warmth_col = column(warmth)
    relax_col = column(relax)
    dens_col = column(picked(populace_ref))
    cold_col = -1.0 / warmth_col
    row_iota = lax.broadcasted_iota(jnp.int32, (rows, LANES), 0)

    def local_piece(c, heat):
        lane = pl.ds(pl.multiple_of(c * LANES, LANES), LANES)
        mom = lax.broadcasted_iota(jnp.int32, (1, LANES), 1) + (me * cols + c * LANES)
        unit = (2.0 * mom.astype(F32) + 1.0) / K - 1.0
        velocity = courant * unit
        energy = energy_top * (unit + energy_shift) ** 2
        for band in range(bands):
            f = grid_ref[band, :, lane]
            below = jnp.where(row_iota == 0, halo_low[band, 7:8, lane], pltpu.roll(f, 1, 0))
            above = jnp.where(
                row_iota == rows - 1, halo_high[band, 0:1, lane], pltpu.roll(f, rows - 1, 0)
            )
            drift = -velocity * jnp.where(velocity > 0, f - below, above - f)
            excess = f - dens_col * jnp.exp((energy + band_offset * band) * cold_col)
            out_ref[band, :, lane] = f + drift - relax_col * excess
            heat = heat + energy * excess
        return heat

    heat = lax.fori_loop(0, pieces, local_piece, jnp.zeros((rows, LANES), F32))
    heat_row = jnp.sum(jnp.transpose(heat), axis=0, keepdims=True)
    heat_send[...] = heat_row
    heat_all[me] = heat_row
    over_peers(lambda peer: heat_copy(peer).start())

    wait_all(pot_all, n_pos - 1, small_recv_sem.at[0])
    wait_all(warmth_all, n_pos - 1, small_recv_sem.at[1])
    n_step = grid_len // FOLD
    base = pos * rows + me * share - HALF
    turn = lax.rem(2 * grid_len - base, grid_len)
    step_iota = lax.broadcasted_iota(jnp.int32, (n_step, grid_len), 0)
    place_iota = lax.broadcasted_iota(jnp.int32, (LANES, LANES), 0)
    lane_iota = lax.broadcasted_iota(jnp.int32, (LANES, LANES), 1)
    signed = jnp.where(lane_iota < LANES // 2, lane_iota, lane_iota - LANES) * FOLD
    for band in range(bands):
        profile = jnp.concatenate(
            [pot_all[j, band : band + 1, :] for j in range(n_pos)], axis=1
        )
        first = profile[:, 0:1]
        last = profile[:, grid_len - 1 : grid_len]
        profile = jnp.broadcast_to(profile, (n_step, grid_len))
        for side in range(2):
            stack = profile
            for m in range(1, n_step):
                shift = (grid_len - FOLD * m) % grid_len if side == 0 else FOLD * m
                stack = jnp.where(step_iota == m, pltpu.roll(profile, shift, 1), stack)
            stack = pltpu.roll(stack, turn, 1)[:, :LANES]
            stack = jnp.transpose(jnp.concatenate([stack] * (LANES // n_step), axis=0))
            index = base + place_iota + (signed if side == 0 else -signed)
            stack = jnp.where(index < 0, first, jnp.where(index > grid_len - 1, last, stack))
            pot_table[band, side] = stack

    scale = potential_gain / K

    def forward_wait(band):
        wait_all(recv.at[band], n_mom - 1, fwd_recv_sem.at[band])

    def transform(band):
        cells = [
            recv[band, j, :, c * LANES : (c + 1) * LANES]
            for j in range(n_mom)
            for c in range(pieces)
        ]
        spec = real_forward(cells)
        for s, (re, im) in enumerate(spec):
            at = pl.ds(s * share, share)
            c_row, s_row = twist_ref[0, s : s + 1, :], twist_ref[1, s : s + 1, :]
            if im is None:
                work[at, :LANES] = re * c_row
                work[at, LANES:] = re * s_row
            else:
                work[at, :LANES] = re * c_row - im * s_row
                work[at, LANES:] = re * s_row + im * c_row
        work[...] = split_dot(work[...], weight_ref[0], weight_ref[1])
        for s in range(HALF + 1):
            at = pl.ds(s * share, share)
            differ = (
                pot_table[band, 0, HALF + s : HALF + s + share, :]
                - pot_table[band, 1, HALF - s : HALF - s + share, :]
            ) * scale
            work[at, :LANES] = work[at, :LANES] * differ
            work[at, LANES:] = work[at, LANES:] * differ
        work[...] = split_dot(work[...], weight_ref[2], weight_ref[3])
        spec = []
        for s in range(HALF + 1):
            at = pl.ds(s * share, share)
            c_row, s_row = twist_ref[0, s : s + 1, :], twist_ref[1, s : s + 1, :]
            re, im = work[at, :LANES], work[at, LANES:]
            spec.append((im * c_row - re * s_row, re * c_row + im * s_row))
        cells = real_inverse(spec)
        for j in range(n_mom):
            for c in range(pieces):
                back_send[band, j, :, c * LANES : (c + 1) * LANES] = cells[j * pieces + c]
        back_recv[band, me] = back_send[band, me]

    def return_start(band):
        over_peers(lambda peer: return_copy(band, peer).start())

    def one_band(band, carry):
        forward_wait(band)

        transform(band)
        return_start(band)
        return carry

    lax.fori_loop(0, bands, one_band, 0)

    def add_back(band, carry):
        wait_all(back_recv.at[band], n_mom - 1, ret_recv_sem.at[band])
        for j in range(n_mom):
            at = pl.ds(j * share, share)
            out_ref[band, at, :] = out_ref[band, at, :] + back_recv[band, j]
        return carry

    lax.fori_loop(0, bands - 1, add_back, 0)

    wait_all(heat_all, n_mom - 1, heat_sem.at[1])
    total = heat_all[0]
    for j in range(1, n_mom):
        total = total + heat_all[j]
    lane_row = lax.broadcasted_iota(jnp.int32, (1, rows), 1)
    low_edge = warmth_all[jnp.maximum(pos - 1, 0), 0:1, rows - 1 : rows]
    high_edge = warmth_all[jnp.minimum(pos + 1, n_pos - 1), 0:1, 0:1]
    low_edge = jnp.where(pos == 0, jnp.ones_like(low_edge), low_edge)
    high_edge = jnp.where(pos == n_pos - 1, jnp.ones_like(high_edge), high_edge)
    before = jnp.where(lane_row == 0, low_edge, pltpu.roll(warmth, 1, 1))
    after = jnp.where(lane_row == rows - 1, high_edge, pltpu.roll(warmth, rows - 1, 1))
    warm_ref[...] = (
        warmth
        + conduct * (after - 2.0 * warmth + before)
        + heat_gain / K * relax * total
        - heat_outflow * (warmth - 1.0)
    )

    wait_all(pot_all, n_pos - 1, small_send_sem.at[0])
    wait_all(warmth_all, n_pos - 1, small_send_sem.at[1])

    @pl.when(pos < n_pos - 1)
    def _():
        halo_copy(True).wait_send()

    @pl.when(pos > 0)
    def _():
        halo_copy(False).wait_send()

    wait_all(heat_all, n_mom - 1, heat_sem.at[0])
    for band in range(bands):
        wait_all(recv.at[band], n_mom - 1, fwd_send_sem.at[band])
        if band < bands - 1:
            wait_all(back_send.at[band], n_mom - 1, ret_send_sem.at[band])
    add_back(bands - 1, 0)
    wait_all(back_send.at[bands - 1], n_mom - 1, ret_send_sem.at[bands - 1])


def write_out(grid_ref, warm_ref, grid_hbm, warm_hbm, sem):
    bands = grid_ref.shape[0]
    copies = [
        pltpu.make_async_copy(grid_ref.at[band], grid_hbm.at[band], sem.at[band])
        for band in range(bands)
    ]
    copies.append(pltpu.make_async_copy(warm_ref, warm_hbm, sem.at[bands]))
    for copy in copies:
        copy.start()
    for copy in copies:
        copy.wait()


def inner_size(n):
    inner = 1
    while inner * inner * 4 <= n:
        inner *= 2
    return inner if n % inner == 0 else 1


def body(
    quasi_probability_grid,
    potential_energy_map,
    contact_inflow_states,
    crystal_kelvin_field,
    area_index_map,
    damping_ratio_per_step,
    equilibrium_populace,
    conductance_per_step,
):
    bands, rows, cols = quasi_probability_grid.shape
    n_pos = lax.axis_size("pos")
    n_mom = lax.axis_size("mom")
    share = rows // n_mom
    kinds = damping_ratio_per_step.shape[0]
    vmem = pl.BlockSpec(memory_space=pltpu.VMEM)
    hbm = pl.BlockSpec(memory_space=pltpu.HBM)
    dma = pltpu.SemaphoreType.DMA
    regular = pltpu.SemaphoreType.REGULAR
    shapes = (
        jax.ShapeDtypeStruct((bands, rows, cols), F32),
        jax.ShapeDtypeStruct((1, rows), F32),
    )
    updated, warm = pl.pallas_call(
        functools.partial(kernel, (bands, rows, cols, n_pos, n_mom)),
        out_shape=shapes,
        in_specs=[hbm] * 8,
        out_specs=(vmem, vmem),
        scratch_shapes=[
            pltpu.VMEM((bands, rows, cols), F32),
            pltpu.VMEM((bands, rows), F32),
            pltpu.VMEM((bands, 2, cols), F32),
            pltpu.VMEM((1, rows), F32),
            pltpu.VMEM((1, rows), jnp.int32),
            pltpu.VMEM((1, kinds), F32),
            pltpu.VMEM((1, kinds), F32),
            pltpu.VMEM((1, kinds), F32),
            pltpu.VMEM((4, 2 * LANES, 2 * LANES), BF16),
            pltpu.VMEM((2, HALF + 8, LANES), F32),
            pltpu.VMEM((bands, n_mom, share, cols), F32),
            pltpu.VMEM((bands, n_mom, share, cols), F32),
            pltpu.VMEM((bands, n_mom, share, cols), F32),
            pltpu.VMEM((bands, 8, cols), F32),
            pltpu.VMEM((bands, 8, cols), F32),
            pltpu.VMEM((n_pos, bands, rows), F32),
            pltpu.VMEM((n_pos, 1, rows), F32),
            pltpu.VMEM((1, rows), F32),
            pltpu.VMEM((n_mom, 1, rows), F32),
            pltpu.VMEM((bands, 2, LANES, LANES), F32),
            pltpu.VMEM(((HALF + 1) * share, 2 * LANES), F32),
            dma((bands,)),
            dma((bands,)),
            dma((bands,)),
            dma((bands,)),
            dma((2,)),
            dma((2,)),
            dma((2,)),
            dma((2,)),
            dma((2,)),
            dma((8,)),
            regular((n_mom // inner_size(n_mom),)),
            regular,
        ],
        compiler_params=pltpu.CompilerParams(
            collective_id=0, has_side_effects=True, vmem_limit_bytes=52 * 1024 * 1024
        ),
    )(
        *(
            pltpu.with_memory_space_constraint(operand, pltpu.HBM)
            for operand in (
                quasi_probability_grid,
                potential_energy_map,
                contact_inflow_states,
                crystal_kelvin_field[None],
                area_index_map[None],
                damping_ratio_per_step[None],
                equilibrium_populace[None],
                conductance_per_step[None],
            )
        )
    )
    updated, warm = pl.pallas_call(
        write_out,
        out_shape=shapes,
        in_specs=[vmem, vmem],
        out_specs=(hbm, hbm),
        scratch_shapes=[dma((bands + 1,))],
        compiler_params=pltpu.CompilerParams(vmem_limit_bytes=8 * 1024 * 1024),
    )(updated, warm)
    return updated, warm[0]


def solution(mesh):
    return jax.shard_map(
        body,
        mesh=mesh,
        in_specs=(
            P(None, "pos", "mom"),
            P(None, "pos"),
            P(None, None, "mom"),
            P("pos"),
            P("pos"),
            P(),
            P(),
            P(),
        ),
        out_specs=(P(None, "pos", "mom"), P("pos")),
        check_vma=False,
    )
```

```python
import functools

import jax
import jax.numpy as jnp
import numpy as np
from jax import lax
from jax.experimental import pallas as pl
from jax.experimental.pallas import tpu as pltpu
from jax.sharding import PartitionSpec as P

K = 8192
LANES = 128
FOLD = K // LANES
HALF = FOLD // 2

courant = 0.9
energy_top = 3.0
energy_shift = 0.25
band_offset = 0.5
potential_gain = 0.5
heat_gain = 0.5
heat_outflow = 0.1

F32 = jnp.float32
BF16 = jnp.bfloat16
MESH = pl.DeviceIdType.MESH


def unit_root(step, length):
    angle = 2.0 * np.pi * step / length
    return float(np.cos(angle)), float(np.sin(angle))


def turned(re, im, c, s):
    if s == 0.0 and c == 1.0:
        return re, im
    if im is None:
        return re * c, re * s
    if abs(c) < 1e-12:
        return -im * s, re * s
    return re * c - im * s, re * s + im * c


def plus(a, b):
    if a is None:
        return b
    if b is None:
        return a
    return a + b


def minus(a, b):
    if b is None:
        return a
    if a is None:
        return -b
    return a - b


def real_forward(xs):
    n = len(xs)
    if n == 2:
        return [(xs[0] + xs[1], None), (xs[0] - xs[1], None)]
    even, odd = real_forward(xs[0::2]), real_forward(xs[1::2])
    out = [None] * (n // 2 + 1)
    for k in range(n // 4 + 1):
        c, s = unit_root(k, n)
        orr, oi = turned(odd[k][0], odd[k][1], c, s)
        er, ei = even[k]
        if 4 * k == n:
            out[k] = (er, odd[k][0])
            continue
        out[k] = (er + orr, plus(ei, oi))
        low = minus(oi, ei)
        out[n // 2 - k] = (er - orr, low)
    return out


def real_inverse(spec):
    n = 2 * (len(spec) - 1)
    if n == 2:
        a, b = spec[0][0], spec[1][0]
        return [a + b, a - b]
    even, odd = [], []
    for k in range(n // 4 + 1):
        ar, ai = spec[k]
        br, bi = spec[n // 2 - k]
        c, s = unit_root(k, n)
        if 4 * k == n:
            even.append((ar + ar, None))
            odd.append((-(ai + ai), None))
            continue
        if k == 0:
            even.append((ar + br, None))
            odd.append((ar - br, None))
            continue
        even.append((ar + br, minus(ai, bi)))
        odd.append(turned(ar - br, plus(ai, bi), c, s))
    xe, xo = real_inverse(even), real_inverse(odd)
    out = [None] * n
    out[0::2], out[1::2] = xe, xo
    return out


def fill_tables(weight_ref, twist_ref):
    row = lax.broadcasted_iota(jnp.int32, (LANES, LANES), 0)
    lane = lax.broadcasted_iota(jnp.int32, (LANES, LANES), 1)
    angle = lax.rem(row * lane, LANES).astype(F32) * (2.0 * np.pi / LANES)
    c, s = jnp.cos(angle), jnp.sin(angle)
    for n, blocks in enumerate((((c, s), (-s, c)), ((c, -s), (s, c)))):
        for a in range(2):
            for b in range(2):
                at = (pl.ds(a * LANES, LANES), pl.ds(b * LANES, LANES))
                high = blocks[a][b].astype(BF16)
                weight_ref[(2 * n,) + at] = high
                weight_ref[(2 * n + 1,) + at] = (blocks[a][b] - high.astype(F32)).astype(BF16)
    count = twist_ref.shape[1]
    angle = (row * lane)[:count].astype(F32) * (2.0 * np.pi / K)
    twist_ref[0] = jnp.cos(angle)
    twist_ref[1] = jnp.sin(angle)


def split_dot(a, high, low):
    a_high = a.astype(BF16)
    a_low = (a - a_high.astype(F32)).astype(BF16)
    dot = functools.partial(jnp.dot, preferred_element_type=F32)
    return dot(a_high, high) + (dot(a_low, high) + dot(a_high, low))


def kernel(
    sizes,
    grid_hbm,
    pot_hbm,
    contact_hbm,
    warmth_hbm,
    area_hbm,
    damping_hbm,
    populace_hbm,
    conduct_hbm,
    out_ref,
    warm_ref,
    grid_ref,
    pot_ref,
    contact_ref,
    warmth_ref,
    area_ref,
    damping_ref,
    populace_ref,
    conduct_ref,
    weight_ref,
    twist_ref,
    recv,
    back_send,
    back_recv,
    halo_low,
    halo_high,
    pot_all,
    warmth_all,
    heat_send,
    heat_all,
    pot_table,
    work,
    fwd_send_sem,
    fwd_recv_sem,
    ret_send_sem,
    ret_recv_sem,
    halo_send_sem,
    halo_recv_sem,
    small_send_sem,
    small_recv_sem,
    heat_sem,
    load_sem,
    mom_ready,
    pos_ready,
):
    bands, rows, cols, n_pos, n_mom = sizes
    share = rows // n_mom
    pieces = cols // LANES
    grid_len = n_pos * rows
    pos = lax.axis_index("pos")
    me = lax.axis_index("mom")

    mom_in = inner_size(n_mom)
    mom_out = n_mom // mom_in
    m_hi, m_lo = me // mom_in, lax.rem(me, mom_in)

    def pos_peer(d):
        return lax.rem(pos + d, n_pos)

    def over_peers(do):
        for d in range(1, n_mom):
            do(lax.rem(me + d, n_mom))

    def wait_all(ref, count, sem):
        block = ref.at[pl.ds(0, count)]
        pltpu.make_async_copy(block, block, sem).wait()

    small = (
        (pot_hbm, pot_ref),
        (contact_hbm, contact_ref),
        (warmth_hbm, warmth_ref),
        (area_hbm, area_ref),
        (damping_hbm, damping_ref),
        (populace_hbm, populace_ref),
        (conduct_hbm, conduct_ref),
    )
    loads = [
        pltpu.make_async_copy(src, dst, load_sem.at[n])
        for n, (src, dst) in enumerate(((grid_hbm, grid_ref),) + small)
    ]

    def small_copy(d, which):
        return pltpu.make_async_remote_copy(
            src_ref=warmth_hbm if which else pot_hbm,
            dst_ref=(warmth_all if which else pot_all).at[pos],
            send_sem=small_send_sem.at[which],
            recv_sem=small_recv_sem.at[which],
            device_id=(pos_peer(d), me),
            device_id_type=MESH,
        )

    def halo_copy(up):
        return pltpu.make_async_remote_copy(
            src_ref=grid_hbm.at[:, pl.ds(rows - 8, 8) if up else pl.ds(0, 8), :],
            dst_ref=halo_low if up else halo_high,
            send_sem=halo_send_sem.at[0 if up else 1],
            recv_sem=halo_recv_sem.at[0 if up else 1],
            device_id=(pos_peer(1 if up else n_pos - 1), me),
            device_id_type=MESH,
        )

    def forward_copy(band, peer):
        return pltpu.make_async_remote_copy(
            src_ref=grid_hbm.at[band, pl.ds(pl.multiple_of(peer * share, share), share), :],
            dst_ref=recv.at[band, me],
            send_sem=fwd_send_sem.at[band],
            recv_sem=fwd_recv_sem.at[band],
            device_id=(pos, peer),
            device_id_type=MESH,
        )

    def return_copy(band, peer):
        return pltpu.make_async_remote_copy(
            src_ref=back_send.at[band, peer],
            dst_ref=back_recv.at[band, me],
            send_sem=ret_send_sem.at[band],
            recv_sem=ret_recv_sem.at[band],
            device_id=(pos, peer),
            device_id_type=MESH,
        )

    def heat_copy(peer):
        return pltpu.make_async_remote_copy(
            src_ref=heat_send,
            dst_ref=heat_all.at[me],
            send_sem=heat_sem.at[0],
            recv_sem=heat_sem.at[1],
            device_id=(pos, peer),
            device_id_type=MESH,
        )

    def start_forward(band, peer):
        forward_copy(band, peer).start()

    for load in loads:
        load.start()

    barrier = pltpu.get_barrier_semaphore()
    for peer in range(1, n_pos):

        @pl.when(pos < peer)
        def _(peer=peer):
            pl.semaphore_signal(barrier, inc=1, device_id=(peer, me), device_id_type=MESH)

    below = (m_hi + mom_out - 1) // mom_out + (m_lo + mom_in - 1) // mom_in + pos

    @pl.when(below > 0)
    def _():
        pl.semaphore_wait(barrier, below)

    @pl.when(m_hi < mom_out - 1)
    def _():
        pl.semaphore_signal(barrier, inc=1, device_id=(pos, me + mom_in), device_id_type=MESH)

    @pl.when(m_lo < mom_in - 1)
    def _():
        pl.semaphore_signal(barrier, inc=1, device_id=(pos, me + 1), device_id_type=MESH)

    def under(peer):
        return (peer // mom_in <= m_hi) & (peer % mom_in <= m_lo) & (peer != me)

    for peer in reversed(range(n_mom - 1)):

        @pl.when(under(peer))
        def _(peer=peer):
            pl.semaphore_signal(
                mom_ready.at[me], inc=1, device_id=(pos, peer), device_id_type=MESH
            )

    for peer in range(n_mom - 1):
        pl.when(under(peer))(functools.partial(start_forward, 0, peer))

    for peer in range(n_pos - 1):

        @pl.when(peer < pos)
        def _(peer=peer):
            pl.semaphore_signal(pos_ready, inc=1, device_id=(peer, me), device_id_type=MESH)

    fill_tables(weight_ref, twist_ref)

    steps = [(i, j) for i in range(mom_out) for j in range(mom_in) if i or j]
    for d_hi, d_lo in sorted(steps, key=lambda step: (sum(step), -step[0])):
        top_hi, top_lo = m_hi + d_hi, m_lo + d_lo
        valid = (top_hi < mom_out) & (top_lo < mom_in)

        @pl.when(valid)
        def _(d_hi=d_hi, d_lo=d_lo, top_hi=top_hi, top_lo=top_lo):
            pl.semaphore_wait(mom_ready.at[top_hi * mom_in + top_lo], 1)
            if d_hi and d_lo:
                start_forward(0, top_hi * mom_in + top_lo)
            elif d_hi:
                for lo in range(mom_in):
                    pl.when(lo <= m_lo)(
                        functools.partial(start_forward, 0, top_hi * mom_in + lo)
                    )
            else:
                for hi in range(mom_out):
                    pl.when(hi <= m_hi)(
                        functools.partial(start_forward, 0, hi * mom_in + top_lo)
                    )

    @pl.when(pos < n_pos - 1)
    def _():
        pl.semaphore_wait(pos_ready, n_pos - 1 - pos)

    for d in range(1, n_pos):
        small_copy(d, 0).start()
        small_copy(d, 1).start()

    @pl.when(pos < n_pos - 1)
    def _():
        halo_copy(True).start()

    @pl.when(pos > 0)
    def _():
        halo_copy(False).start()

    for band in range(1, bands):
        over_peers(functools.partial(start_forward, band))
    for load in loads:
        load.wait()

    own = pl.ds(pl.multiple_of(me * share, share), share)
    for band in range(bands):
        recv[band, me] = grid_ref[band, own, :]
    pot_all[pos] = pot_ref[...]
    warmth_all[pos] = warmth_ref[...]

    @pl.when(pos == 0)
    def _():
        halo_low[:, 7:8, :] = contact_ref[:, 0:1, :]

    @pl.when(pos > 0)
    def _():
        halo_copy(True).wait_recv()

    @pl.when(pos == n_pos - 1)
    def _():
        halo_high[:, 0:1, :] = contact_ref[:, 1:2, :]

    @pl.when(pos < n_pos - 1)
    def _():
        halo_copy(False).wait_recv()

    def picked(values):
        total = jnp.zeros((1, rows), F32)
        for n in range(values.shape[1]):
            total = jnp.where(area_ref[...] == n, values[0:1, n : n + 1], total)
        return total

    def column(row):
        return jnp.transpose(jnp.broadcast_to(row, (rows, rows)))

    warmth = warmth_ref[...]
    relax = picked(damping_ref)
    conduct = picked(conduct_ref)
    warmth_col = column(warmth)
    relax_col = column(relax)
    dens_col = column(picked(populace_ref))
    cold_col = -1.0 / warmth_col
    row_iota = lax.broadcasted_iota(jnp.int32, (rows, LANES), 0)

    def local_piece(c, heat):
        lane = pl.ds(pl.multiple_of(c * LANES, LANES), LANES)
        mom = lax.broadcasted_iota(jnp.int32, (1, LANES), 1) + (me * cols + c * LANES)
        unit = (2.0 * mom.astype(F32) + 1.0) / K - 1.0
        velocity = courant * unit
        energy = energy_top * (unit + energy_shift) ** 2
        for band in range(bands):
            f = grid_ref[band, :, lane]
            below = jnp.where(row_iota == 0, halo_low[band, 7:8, lane], pltpu.roll(f, 1, 0))
            above = jnp.where(
                row_iota == rows - 1, halo_high[band, 0:1, lane], pltpu.roll(f, rows - 1, 0)
            )
            drift = -velocity * jnp.where(velocity > 0, f - below, above - f)
            excess = f - dens_col * jnp.exp((energy + band_offset * band) * cold_col)
            out_ref[band, :, lane] = f + drift - relax_col * excess
            heat = heat + energy * excess
        return heat

    heat = lax.fori_loop(0, pieces, local_piece, jnp.zeros((rows, LANES), F32))
    heat_row = jnp.sum(jnp.transpose(heat), axis=0, keepdims=True)
    heat_send[...] = heat_row
    heat_all[me] = heat_row
    over_peers(lambda peer: heat_copy(peer).start())

    wait_all(pot_all, n_pos - 1, small_recv_sem.at[0])
    wait_all(warmth_all, n_pos - 1, small_recv_sem.at[1])
    n_step = grid_len // FOLD
    base = pos * rows + me * share - HALF
    turn = lax.rem(2 * grid_len - base, grid_len)
    step_iota = lax.broadcasted_iota(jnp.int32, (n_step, grid_len), 0)
    place_iota = lax.broadcasted_iota(jnp.int32, (LANES, LANES), 0)
    lane_iota = lax.broadcasted_iota(jnp.int32, (LANES, LANES), 1)
    signed = jnp.where(lane_iota < LANES // 2, lane_iota, lane_iota - LANES) * FOLD
    for band in range(bands):
        profile = jnp.concatenate(
            [pot_all[j, band : band + 1, :] for j in range(n_pos)], axis=1
        )
        first = profile[:, 0:1]
        last = profile[:, grid_len - 1 : grid_len]
        profile = jnp.broadcast_to(profile, (n_step, grid_len))
        for side in range(2):
            stack = profile
            for m in range(1, n_step):
                shift = (grid_len - FOLD * m) % grid_len if side == 0 else FOLD * m
                stack = jnp.where(step_iota == m, pltpu.roll(profile, shift, 1), stack)
            stack = pltpu.roll(stack, turn, 1)[:, :LANES]
            stack = jnp.transpose(jnp.concatenate([stack] * (LANES // n_step), axis=0))
            index = base + place_iota + (signed if side == 0 else -signed)
            stack = jnp.where(index < 0, first, jnp.where(index > grid_len - 1, last, stack))
            pot_table[band, side] = stack

    scale = potential_gain / K

    def forward_wait(band):
        wait_all(recv.at[band], n_mom - 1, fwd_recv_sem.at[band])

    def transform(band):
        cells = [
            recv[band, j, :, c * LANES : (c + 1) * LANES]
            for j in range(n_mom)
            for c in range(pieces)
        ]
        spec = real_forward(cells)
        for s, (re, im) in enumerate(spec):
            at = pl.ds(s * share, share)
            c_row, s_row = twist_ref[0, s : s + 1, :], twist_ref[1, s : s + 1, :]
            if im is None:
                work[at, :LANES] = re * c_row
                work[at, LANES:] = re * s_row
            else:
                work[at, :LANES] = re * c_row - im * s_row
                work[at, LANES:] = re * s_row + im * c_row
        work[...] = split_dot(work[...], weight_ref[0], weight_ref[1])
        for s in range(HALF + 1):
            at = pl.ds(s * share, share)
            differ = (
                pot_table[band, 0, HALF + s : HALF + s + share, :]
                - pot_table[band, 1, HALF - s : HALF - s + share, :]
            ) * scale
            work[at, :LANES] = work[at, :LANES] * differ
            work[at, LANES:] = work[at, LANES:] * differ
        work[...] = split_dot(work[...], weight_ref[2], weight_ref[3])
        spec = []
        for s in range(HALF + 1):
            at = pl.ds(s * share, share)
            c_row, s_row = twist_ref[0, s : s + 1, :], twist_ref[1, s : s + 1, :]
            re, im = work[at, :LANES], work[at, LANES:]
            spec.append((im * c_row - re * s_row, re * c_row + im * s_row))
        cells = real_inverse(spec)
        for j in range(n_mom):
            for c in range(pieces):
                back_send[band, j, :, c * LANES : (c + 1) * LANES] = cells[j * pieces + c]
        back_recv[band, me] = back_send[band, me]

    def return_start(band):
        over_peers(lambda peer: return_copy(band, peer).start())

    def one_band(band, carry):
        forward_wait(band)

        transform(band)
        return_start(band)
        return carry

    lax.fori_loop(0, bands, one_band, 0)

    def add_back(band, carry):
        wait_all(back_recv.at[band], n_mom - 1, ret_recv_sem.at[band])
        for j in range(n_mom):
            at = pl.ds(j * share, share)
            out_ref[band, at, :] = out_ref[band, at, :] + back_recv[band, j]
        return carry

    lax.fori_loop(0, bands - 1, add_back, 0)

    wait_all(heat_all, n_mom - 1, heat_sem.at[1])
    total = heat_all[0]
    for j in range(1, n_mom):
        total = total + heat_all[j]
    lane_row = lax.broadcasted_iota(jnp.int32, (1, rows), 1)
    low_edge = warmth_all[jnp.maximum(pos - 1, 0), 0:1, rows - 1 : rows]
    high_edge = warmth_all[jnp.minimum(pos + 1, n_pos - 1), 0:1, 0:1]
    low_edge = jnp.where(pos == 0, jnp.ones_like(low_edge), low_edge)
    high_edge = jnp.where(pos == n_pos - 1, jnp.ones_like(high_edge), high_edge)
    before = jnp.where(lane_row == 0, low_edge, pltpu.roll(warmth, 1, 1))
    after = jnp.where(lane_row == rows - 1, high_edge, pltpu.roll(warmth, rows - 1, 1))
    warm_ref[...] = (
        warmth
        + conduct * (after - 2.0 * warmth + before)
        + heat_gain / K * relax * total
        - heat_outflow * (warmth - 1.0)
    )

    wait_all(pot_all, n_pos - 1, small_send_sem.at[0])
    wait_all(warmth_all, n_pos - 1, small_send_sem.at[1])

    @pl.when(pos < n_pos - 1)
    def _():
        halo_copy(True).wait_send()

    @pl.when(pos > 0)
    def _():
        halo_copy(False).wait_send()

    wait_all(heat_all, n_mom - 1, heat_sem.at[0])
    for band in range(bands):
        wait_all(recv.at[band], n_mom - 1, fwd_send_sem.at[band])
        if band < bands - 1:
            wait_all(back_send.at[band], n_mom - 1, ret_send_sem.at[band])
    add_back(bands - 1, 0)
    wait_all(back_send.at[bands - 1], n_mom - 1, ret_send_sem.at[bands - 1])


def write_out(grid_ref, warm_ref, grid_hbm, warm_hbm, sem):
    bands = grid_ref.shape[0]
    copies = [
        pltpu.make_async_copy(grid_ref.at[band], grid_hbm.at[band], sem.at[band])
        for band in range(bands)
    ]
    copies.append(pltpu.make_async_copy(warm_ref, warm_hbm, sem.at[bands]))
    for copy in copies:
        copy.start()
    for copy in copies:
        copy.wait()


def inner_size(n):
    inner = 1
    while inner * inner * 4 <= n:
        inner *= 2
    return inner if n % inner == 0 else 1


def body(
    quasi_probability_grid,
    potential_energy_map,
    contact_inflow_states,
    crystal_kelvin_field,
    area_index_map,
    damping_ratio_per_step,
    equilibrium_populace,
    conductance_per_step,
):
    bands, rows, cols = quasi_probability_grid.shape
    n_pos = lax.axis_size("pos")
    n_mom = lax.axis_size("mom")
    share = rows // n_mom
    kinds = damping_ratio_per_step.shape[0]
    vmem = pl.BlockSpec(memory_space=pltpu.VMEM)
    hbm = pl.BlockSpec(memory_space=pltpu.HBM)
    dma = pltpu.SemaphoreType.DMA
    regular = pltpu.SemaphoreType.REGULAR
    shapes = (
        jax.ShapeDtypeStruct((bands, rows, cols), F32),
        jax.ShapeDtypeStruct((1, rows), F32),
    )
    updated, warm = pl.pallas_call(
        functools.partial(kernel, (bands, rows, cols, n_pos, n_mom)),
        out_shape=shapes,
        in_specs=[hbm] * 8,
        out_specs=(vmem, vmem),
        scratch_shapes=[
            pltpu.VMEM((bands, rows, cols), F32),
            pltpu.VMEM((bands, rows), F32),
            pltpu.VMEM((bands, 2, cols), F32),
            pltpu.VMEM((1, rows), F32),
            pltpu.VMEM((1, rows), jnp.int32),
            pltpu.VMEM((1, kinds), F32),
            pltpu.VMEM((1, kinds), F32),
            pltpu.VMEM((1, kinds), F32),
            pltpu.VMEM((4, 2 * LANES, 2 * LANES), BF16),
            pltpu.VMEM((2, HALF + 8, LANES), F32),
            pltpu.VMEM((bands, n_mom, share, cols), F32),
            pltpu.VMEM((bands, n_mom, share, cols), F32),
            pltpu.VMEM((bands, n_mom, share, cols), F32),
            pltpu.VMEM((bands, 8, cols), F32),
            pltpu.VMEM((bands, 8, cols), F32),
            pltpu.VMEM((n_pos, bands, rows), F32),
            pltpu.VMEM((n_pos, 1, rows), F32),
            pltpu.VMEM((1, rows), F32),
            pltpu.VMEM((n_mom, 1, rows), F32),
            pltpu.VMEM((bands, 2, LANES, LANES), F32),
            pltpu.VMEM(((HALF + 1) * share, 2 * LANES), F32),
            dma((bands,)),
            dma((bands,)),
            dma((bands,)),
            dma((bands,)),
            dma((2,)),
            dma((2,)),
            dma((2,)),
            dma((2,)),
            dma((2,)),
            dma((8,)),
            regular((n_mom,)),
            regular,
        ],
        compiler_params=pltpu.CompilerParams(
            collective_id=0, has_side_effects=True, vmem_limit_bytes=52 * 1024 * 1024
        ),
    )(
        *(
            pltpu.with_memory_space_constraint(operand, pltpu.HBM)
            for operand in (
                quasi_probability_grid,
                potential_energy_map,
                contact_inflow_states,
                crystal_kelvin_field[None],
                area_index_map[None],
                damping_ratio_per_step[None],
                equilibrium_populace[None],
                conductance_per_step[None],
            )
        )
    )
    updated, warm = pl.pallas_call(
        write_out,
        out_shape=shapes,
        in_specs=[vmem, vmem],
        out_specs=(hbm, hbm),
        scratch_shapes=[dma((bands + 1,))],
        compiler_params=pltpu.CompilerParams(vmem_limit_bytes=8 * 1024 * 1024),
    )(updated, warm)
    return updated, warm[0]


def solution(mesh):
    return jax.shard_map(
        body,
        mesh=mesh,
        in_specs=(
            P(None, "pos", "mom"),
            P(None, "pos"),
            P(None, None, "mom"),
            P("pos"),
            P("pos"),
            P(),
            P(),
            P(),
        ),
        out_specs=(P(None, "pos", "mom"), P("pos")),
        check_vma=False,
    )
```

```python
import functools

import jax
import jax.numpy as jnp
import numpy as np
from jax import lax
from jax.experimental import pallas as pl
from jax.experimental.pallas import tpu as pltpu
from jax.sharding import PartitionSpec as P

K = 8192
LANES = 128
FOLD = K // LANES
HALF = FOLD // 2

courant = 0.9
energy_top = 3.0
energy_shift = 0.25
band_offset = 0.5
potential_gain = 0.5
heat_gain = 0.5
heat_outflow = 0.1

F32 = jnp.float32
BF16 = jnp.bfloat16
MESH = pl.DeviceIdType.MESH


def unit_root(step, length):
    angle = 2.0 * np.pi * step / length
    return float(np.cos(angle)), float(np.sin(angle))


def turned(re, im, c, s):
    if s == 0.0 and c == 1.0:
        return re, im
    if im is None:
        return re * c, re * s
    if abs(c) < 1e-12:
        return -im * s, re * s
    return re * c - im * s, re * s + im * c


def plus(a, b):
    if a is None:
        return b
    if b is None:
        return a
    return a + b


def minus(a, b):
    if b is None:
        return a
    if a is None:
        return -b
    return a - b


def real_forward(xs):
    n = len(xs)
    if n == 2:
        return [(xs[0] + xs[1], None), (xs[0] - xs[1], None)]
    even, odd = real_forward(xs[0::2]), real_forward(xs[1::2])
    out = [None] * (n // 2 + 1)
    for k in range(n // 4 + 1):
        c, s = unit_root(k, n)
        orr, oi = turned(odd[k][0], odd[k][1], c, s)
        er, ei = even[k]
        if 4 * k == n:
            out[k] = (er, odd[k][0])
            continue
        out[k] = (er + orr, plus(ei, oi))
        low = minus(oi, ei)
        out[n // 2 - k] = (er - orr, low)
    return out


def real_inverse(spec):
    n = 2 * (len(spec) - 1)
    if n == 2:
        a, b = spec[0][0], spec[1][0]
        return [a + b, a - b]
    even, odd = [], []
    for k in range(n // 4 + 1):
        ar, ai = spec[k]
        br, bi = spec[n // 2 - k]
        c, s = unit_root(k, n)
        if 4 * k == n:
            even.append((ar + ar, None))
            odd.append((-(ai + ai), None))
            continue
        if k == 0:
            even.append((ar + br, None))
            odd.append((ar - br, None))
            continue
        even.append((ar + br, minus(ai, bi)))
        odd.append(turned(ar - br, plus(ai, bi), c, s))
    xe, xo = real_inverse(even), real_inverse(odd)
    out = [None] * n
    out[0::2], out[1::2] = xe, xo
    return out


def fill_tables(weight_ref, twist_ref):
    row = lax.broadcasted_iota(jnp.int32, (LANES, LANES), 0)
    lane = lax.broadcasted_iota(jnp.int32, (LANES, LANES), 1)
    angle = lax.rem(row * lane, LANES).astype(F32) * (2.0 * np.pi / LANES)
    c, s = jnp.cos(angle), jnp.sin(angle)
    for n, blocks in enumerate((((c, s), (-s, c)), ((c, -s), (s, c)))):
        for a in range(2):
            for b in range(2):
                at = (pl.ds(a * LANES, LANES), pl.ds(b * LANES, LANES))
                high = blocks[a][b].astype(BF16)
                weight_ref[(2 * n,) + at] = high
                weight_ref[(2 * n + 1,) + at] = (blocks[a][b] - high.astype(F32)).astype(BF16)
    count = twist_ref.shape[1]
    angle = (row * lane)[:count].astype(F32) * (2.0 * np.pi / K)
    twist_ref[0] = jnp.cos(angle)
    twist_ref[1] = jnp.sin(angle)


def split_dot(a, high, low):
    a_high = a.astype(BF16)
    a_low = (a - a_high.astype(F32)).astype(BF16)
    dot = functools.partial(jnp.dot, preferred_element_type=F32)
    return dot(a_high, high) + (dot(a_low, high) + dot(a_high, low))


def kernel(
    sizes,
    grid_hbm,
    pot_hbm,
    contact_hbm,
    warmth_hbm,
    area_hbm,
    damping_hbm,
    populace_hbm,
    conduct_hbm,
    out_ref,
    warm_ref,
    grid_ref,
    pot_ref,
    contact_ref,
    warmth_ref,
    area_ref,
    damping_ref,
    populace_ref,
    conduct_ref,
    weight_ref,
    twist_ref,
    recv,
    back_send,
    back_recv,
    halo_low,
    halo_high,
    pot_all,
    warmth_all,
    heat_send,
    heat_all,
    pot_table,
    work,
    fwd_send_sem,
    fwd_recv_sem,
    ret_send_sem,
    ret_recv_sem,
    halo_send_sem,
    halo_recv_sem,
    small_send_sem,
    small_recv_sem,
    heat_sem,
    load_sem,
    mom_ready,
    pos_ready,
):
    bands, rows, cols, n_pos, n_mom = sizes
    share = rows // n_mom
    pieces = cols // LANES
    grid_len = n_pos * rows
    pos = lax.axis_index("pos")
    me = lax.axis_index("mom")

    mom_in = inner_size(n_mom)
    mom_out = n_mom // mom_in
    m_hi, m_lo = me // mom_in, lax.rem(me, mom_in)

    def pos_peer(d):
        return lax.rem(pos + d, n_pos)

    def over_peers(do):
        for d in range(1, n_mom):
            do(lax.rem(me + d, n_mom))

    def wait_all(ref, count, sem):
        block = ref.at[pl.ds(0, count)]
        pltpu.make_async_copy(block, block, sem).wait()

    small = (
        (pot_hbm, pot_ref),
        (contact_hbm, contact_ref),
        (warmth_hbm, warmth_ref),
        (area_hbm, area_ref),
        (damping_hbm, damping_ref),
        (populace_hbm, populace_ref),
        (conduct_hbm, conduct_ref),
    )
    loads = [
        pltpu.make_async_copy(src, dst, load_sem.at[n])
        for n, (src, dst) in enumerate(((grid_hbm, grid_ref),) + small)
    ]

    def small_copy(d, which):
        return pltpu.make_async_remote_copy(
            src_ref=warmth_hbm if which else pot_hbm,
            dst_ref=(warmth_all if which else pot_all).at[pos],
            send_sem=small_send_sem.at[which],
            recv_sem=small_recv_sem.at[which],
            device_id=(pos_peer(d), me),
            device_id_type=MESH,
        )

    def halo_copy(up):
        return pltpu.make_async_remote_copy(
            src_ref=grid_hbm.at[:, pl.ds(rows - 8, 8) if up else pl.ds(0, 8), :],
            dst_ref=halo_low if up else halo_high,
            send_sem=halo_send_sem.at[0 if up else 1],
            recv_sem=halo_recv_sem.at[0 if up else 1],
            device_id=(pos_peer(1 if up else n_pos - 1), me),
            device_id_type=MESH,
        )

    def forward_copy(band, peer):
        return pltpu.make_async_remote_copy(
            src_ref=grid_hbm.at[band, pl.ds(pl.multiple_of(peer * share, share), share), :],
            dst_ref=recv.at[band, me],
            send_sem=fwd_send_sem.at[band],
            recv_sem=fwd_recv_sem.at[band],
            device_id=(pos, peer),
            device_id_type=MESH,
        )

    def return_copy(band, peer):
        return pltpu.make_async_remote_copy(
            src_ref=back_send.at[band, peer],
            dst_ref=back_recv.at[band, me],
            send_sem=ret_send_sem.at[band],
            recv_sem=ret_recv_sem.at[band],
            device_id=(pos, peer),
            device_id_type=MESH,
        )

    def heat_copy(peer):
        return pltpu.make_async_remote_copy(
            src_ref=heat_send,
            dst_ref=heat_all.at[me],
            send_sem=heat_sem.at[0],
            recv_sem=heat_sem.at[1],
            device_id=(pos, peer),
            device_id_type=MESH,
        )

    def start_forward(band, peer):
        forward_copy(band, peer).start()

    for load in loads:
        load.start()

    def under(peer):
        return (peer // mom_in <= m_hi) & (peer % mom_in <= m_lo) & (peer != me)

    def over(peer):
        return (peer // mom_in >= m_hi) & (peer % mom_in >= m_lo) & (peer != me)

    upper_row = mom_out // 2 if mom_out % 2 == 0 else mom_out
    at_middle = m_hi == upper_row - 1 if mom_out % 2 == 0 else m_hi < 0
    barrier = pltpu.get_barrier_semaphore()

    @pl.when(m_hi == upper_row)
    def _():
        pl.semaphore_signal(barrier, inc=1, device_id=(pos, me - mom_in), device_id_type=MESH)

    for peer in range(1, n_mom):

        @pl.when(over(peer))
        def _(peer=peer):
            pl.semaphore_signal(barrier, inc=1, device_id=(pos, peer), device_id_type=MESH)

    for peer in range(1, n_pos):

        @pl.when(pos < peer)
        def _(peer=peer):
            pl.semaphore_signal(barrier, inc=1, device_id=(peer, me), device_id_type=MESH)

    below = (m_hi + 1) * (m_lo + 1) - 1 + pos + jnp.where(at_middle, 1, 0)

    @pl.when(below > 0)
    def _():
        pl.semaphore_wait(barrier, below)

    @pl.when(at_middle)
    def _():
        start_forward(0, me + mom_in)

    for peer in reversed(range(n_mom - 1)):

        @pl.when(under(peer))
        def _(peer=peer):
            pl.semaphore_signal(
                mom_ready.at[me], inc=1, device_id=(pos, peer), device_id_type=MESH
            )

    for peer in range(n_mom - 1):
        pl.when(under(peer))(functools.partial(start_forward, 0, peer))

    for peer in range(n_pos - 1):

        @pl.when(peer < pos)
        def _(peer=peer):
            pl.semaphore_signal(pos_ready, inc=1, device_id=(peer, me), device_id_type=MESH)

    fill_tables(weight_ref, twist_ref)

    steps = [(i, j) for i in range(mom_out) for j in range(mom_in) if i or j]
    for d_hi, d_lo in sorted(steps, key=lambda step: (sum(step), -step[0])):
        top_hi, top_lo = m_hi + d_hi, m_lo + d_lo
        valid = (top_hi < mom_out) & (top_lo < mom_in)

        @pl.when(valid)
        def _(d_hi=d_hi, d_lo=d_lo, top_hi=top_hi, top_lo=top_lo):
            pl.semaphore_wait(mom_ready.at[top_hi * mom_in + top_lo], 1)
            if d_hi and d_lo:
                start_forward(0, top_hi * mom_in + top_lo)
            elif d_hi:
                for lo in range(mom_in):
                    done = at_middle & (lo == m_lo) if d_hi == 1 else lo < 0
                    pl.when((lo <= m_lo) & jnp.logical_not(done))(
                        functools.partial(start_forward, 0, top_hi * mom_in + lo)
                    )
            else:
                for hi in range(mom_out):
                    pl.when(hi <= m_hi)(
                        functools.partial(start_forward, 0, hi * mom_in + top_lo)
                    )

    @pl.when(pos < n_pos - 1)
    def _():
        pl.semaphore_wait(pos_ready, n_pos - 1 - pos)

    for d in range(1, n_pos):
        small_copy(d, 0).start()
        small_copy(d, 1).start()

    @pl.when(pos < n_pos - 1)
    def _():
        halo_copy(True).start()

    @pl.when(pos > 0)
    def _():
        halo_copy(False).start()

    for band in range(1, bands):
        over_peers(functools.partial(start_forward, band))
    for load in loads:
        load.wait()

    own = pl.ds(pl.multiple_of(me * share, share), share)
    for band in range(bands):
        recv[band, me] = grid_ref[band, own, :]
    pot_all[pos] = pot_ref[...]
    warmth_all[pos] = warmth_ref[...]

    @pl.when(pos == 0)
    def _():
        halo_low[:, 7:8, :] = contact_ref[:, 0:1, :]

    @pl.when(pos > 0)
    def _():
        halo_copy(True).wait_recv()

    @pl.when(pos == n_pos - 1)
    def _():
        halo_high[:, 0:1, :] = contact_ref[:, 1:2, :]

    @pl.when(pos < n_pos - 1)
    def _():
        halo_copy(False).wait_recv()

    def picked(values):
        total = jnp.zeros((1, rows), F32)
        for n in range(values.shape[1]):
            total = jnp.where(area_ref[...] == n, values[0:1, n : n + 1], total)
        return total

    def column(row):
        return jnp.transpose(jnp.broadcast_to(row, (rows, rows)))

    warmth = warmth_ref[...]
    relax = picked(damping_ref)
    conduct = picked(conduct_ref)
    warmth_col = column(warmth)
    relax_col = column(relax)
    dens_col = column(picked(populace_ref))
    cold_col = -1.0 / warmth_col
    row_iota = lax.broadcasted_iota(jnp.int32, (rows, LANES), 0)

    def local_piece(c, heat):
        lane = pl.ds(pl.multiple_of(c * LANES, LANES), LANES)
        mom = lax.broadcasted_iota(jnp.int32, (1, LANES), 1) + (me * cols + c * LANES)
        unit = (2.0 * mom.astype(F32) + 1.0) / K - 1.0
        velocity = courant * unit
        energy = energy_top * (unit + energy_shift) ** 2
        for band in range(bands):
            f = grid_ref[band, :, lane]
            below = jnp.where(row_iota == 0, halo_low[band, 7:8, lane], pltpu.roll(f, 1, 0))
            above = jnp.where(
                row_iota == rows - 1, halo_high[band, 0:1, lane], pltpu.roll(f, rows - 1, 0)
            )
            drift = -velocity * jnp.where(velocity > 0, f - below, above - f)
            excess = f - dens_col * jnp.exp((energy + band_offset * band) * cold_col)
            out_ref[band, :, lane] = f + drift - relax_col * excess
            heat = heat + energy * excess
        return heat

    heat = lax.fori_loop(0, pieces, local_piece, jnp.zeros((rows, LANES), F32))
    heat_row = jnp.sum(jnp.transpose(heat), axis=0, keepdims=True)
    heat_send[...] = heat_row
    heat_all[me] = heat_row
    over_peers(lambda peer: heat_copy(peer).start())

    wait_all(pot_all, n_pos - 1, small_recv_sem.at[0])
    wait_all(warmth_all, n_pos - 1, small_recv_sem.at[1])
    n_step = grid_len // FOLD
    base = pos * rows + me * share - HALF
    turn = lax.rem(2 * grid_len - base, grid_len)
    step_iota = lax.broadcasted_iota(jnp.int32, (n_step, grid_len), 0)
    place_iota = lax.broadcasted_iota(jnp.int32, (LANES, LANES), 0)
    lane_iota = lax.broadcasted_iota(jnp.int32, (LANES, LANES), 1)
    signed = jnp.where(lane_iota < LANES // 2, lane_iota, lane_iota - LANES) * FOLD
    for band in range(bands):
        profile = jnp.concatenate(
            [pot_all[j, band : band + 1, :] for j in range(n_pos)], axis=1
        )
        first = profile[:, 0:1]
        last = profile[:, grid_len - 1 : grid_len]
        profile = jnp.broadcast_to(profile, (n_step, grid_len))
        for side in range(2):
            stack = profile
            for m in range(1, n_step):
                shift = (grid_len - FOLD * m) % grid_len if side == 0 else FOLD * m
                stack = jnp.where(step_iota == m, pltpu.roll(profile, shift, 1), stack)
            stack = pltpu.roll(stack, turn, 1)[:, :LANES]
            stack = jnp.transpose(jnp.concatenate([stack] * (LANES // n_step), axis=0))
            index = base + place_iota + (signed if side == 0 else -signed)
            stack = jnp.where(index < 0, first, jnp.where(index > grid_len - 1, last, stack))
            pot_table[band, side] = stack

    scale = potential_gain / K

    def forward_wait(band):
        wait_all(recv.at[band], n_mom - 1, fwd_recv_sem.at[band])

    def transform(band):
        cells = [
            recv[band, j, :, c * LANES : (c + 1) * LANES]
            for j in range(n_mom)
            for c in range(pieces)
        ]
        spec = real_forward(cells)
        for s, (re, im) in enumerate(spec):
            at = pl.ds(s * share, share)
            c_row, s_row = twist_ref[0, s : s + 1, :], twist_ref[1, s : s + 1, :]
            if im is None:
                work[at, :LANES] = re * c_row
                work[at, LANES:] = re * s_row
            else:
                work[at, :LANES] = re * c_row - im * s_row
                work[at, LANES:] = re * s_row + im * c_row
        work[...] = split_dot(work[...], weight_ref[0], weight_ref[1])
        for s in range(HALF + 1):
            at = pl.ds(s * share, share)
            differ = (
                pot_table[band, 0, HALF + s : HALF + s + share, :]
                - pot_table[band, 1, HALF - s : HALF - s + share, :]
            ) * scale
            work[at, :LANES] = work[at, :LANES] * differ
            work[at, LANES:] = work[at, LANES:] * differ
        work[...] = split_dot(work[...], weight_ref[2], weight_ref[3])
        spec = []
        for s in range(HALF + 1):
            at = pl.ds(s * share, share)
            c_row, s_row = twist_ref[0, s : s + 1, :], twist_ref[1, s : s + 1, :]
            re, im = work[at, :LANES], work[at, LANES:]
            spec.append((im * c_row - re * s_row, re * c_row + im * s_row))
        cells = real_inverse(spec)
        for j in range(n_mom):
            for c in range(pieces):
                back_send[band, j, :, c * LANES : (c + 1) * LANES] = cells[j * pieces + c]
        back_recv[band, me] = back_send[band, me]

    def return_start(band):
        over_peers(lambda peer: return_copy(band, peer).start())

    def one_band(band, carry):
        forward_wait(band)

        transform(band)
        return_start(band)
        return carry

    lax.fori_loop(0, bands, one_band, 0)

    def add_back(band, carry):
        wait_all(back_recv.at[band], n_mom - 1, ret_recv_sem.at[band])
        for j in range(n_mom):
            at = pl.ds(j * share, share)
            out_ref[band, at, :] = out_ref[band, at, :] + back_recv[band, j]
        return carry

    lax.fori_loop(0, bands - 1, add_back, 0)

    wait_all(heat_all, n_mom - 1, heat_sem.at[1])
    total = heat_all[0]
    for j in range(1, n_mom):
        total = total + heat_all[j]
    lane_row = lax.broadcasted_iota(jnp.int32, (1, rows), 1)
    low_edge = warmth_all[jnp.maximum(pos - 1, 0), 0:1, rows - 1 : rows]
    high_edge = warmth_all[jnp.minimum(pos + 1, n_pos - 1), 0:1, 0:1]
    low_edge = jnp.where(pos == 0, jnp.ones_like(low_edge), low_edge)
    high_edge = jnp.where(pos == n_pos - 1, jnp.ones_like(high_edge), high_edge)
    before = jnp.where(lane_row == 0, low_edge, pltpu.roll(warmth, 1, 1))
    after = jnp.where(lane_row == rows - 1, high_edge, pltpu.roll(warmth, rows - 1, 1))
    warm_ref[...] = (
        warmth
        + conduct * (after - 2.0 * warmth + before)
        + heat_gain / K * relax * total
        - heat_outflow * (warmth - 1.0)
    )

    wait_all(pot_all, n_pos - 1, small_send_sem.at[0])
    wait_all(warmth_all, n_pos - 1, small_send_sem.at[1])

    @pl.when(pos < n_pos - 1)
    def _():
        halo_copy(True).wait_send()

    @pl.when(pos > 0)
    def _():
        halo_copy(False).wait_send()

    wait_all(heat_all, n_mom - 1, heat_sem.at[0])
    for band in range(bands):
        wait_all(recv.at[band], n_mom - 1, fwd_send_sem.at[band])
        if band < bands - 1:
            wait_all(back_send.at[band], n_mom - 1, ret_send_sem.at[band])
    add_back(bands - 1, 0)
    wait_all(back_send.at[bands - 1], n_mom - 1, ret_send_sem.at[bands - 1])


def write_out(grid_ref, warm_ref, grid_hbm, warm_hbm, sem):
    bands = grid_ref.shape[0]
    copies = [
        pltpu.make_async_copy(grid_ref.at[band], grid_hbm.at[band], sem.at[band])
        for band in range(bands)
    ]
    copies.append(pltpu.make_async_copy(warm_ref, warm_hbm, sem.at[bands]))
    for copy in copies:
        copy.start()
    for copy in copies:
        copy.wait()


def inner_size(n):
    inner = 1
    while inner * inner * 4 <= n:
        inner *= 2
    return inner if n % inner == 0 else 1


def body(
    quasi_probability_grid,
    potential_energy_map,
    contact_inflow_states,
    crystal_kelvin_field,
    area_index_map,
    damping_ratio_per_step,
    equilibrium_populace,
    conductance_per_step,
):
    bands, rows, cols = quasi_probability_grid.shape
    n_pos = lax.axis_size("pos")
    n_mom = lax.axis_size("mom")
    share = rows // n_mom
    kinds = damping_ratio_per_step.shape[0]
    vmem = pl.BlockSpec(memory_space=pltpu.VMEM)
    hbm = pl.BlockSpec(memory_space=pltpu.HBM)
    dma = pltpu.SemaphoreType.DMA
    regular = pltpu.SemaphoreType.REGULAR
    shapes = (
        jax.ShapeDtypeStruct((bands, rows, cols), F32),
        jax.ShapeDtypeStruct((1, rows), F32),
    )
    updated, warm = pl.pallas_call(
        functools.partial(kernel, (bands, rows, cols, n_pos, n_mom)),
        out_shape=shapes,
        in_specs=[hbm] * 8,
        out_specs=(vmem, vmem),
        scratch_shapes=[
            pltpu.VMEM((bands, rows, cols), F32),
            pltpu.VMEM((bands, rows), F32),
            pltpu.VMEM((bands, 2, cols), F32),
            pltpu.VMEM((1, rows), F32),
            pltpu.VMEM((1, rows), jnp.int32),
            pltpu.VMEM((1, kinds), F32),
            pltpu.VMEM((1, kinds), F32),
            pltpu.VMEM((1, kinds), F32),
            pltpu.VMEM((4, 2 * LANES, 2 * LANES), BF16),
            pltpu.VMEM((2, HALF + 8, LANES), F32),
            pltpu.VMEM((bands, n_mom, share, cols), F32),
            pltpu.VMEM((bands, n_mom, share, cols), F32),
            pltpu.VMEM((bands, n_mom, share, cols), F32),
            pltpu.VMEM((bands, 8, cols), F32),
            pltpu.VMEM((bands, 8, cols), F32),
            pltpu.VMEM((n_pos, bands, rows), F32),
            pltpu.VMEM((n_pos, 1, rows), F32),
            pltpu.VMEM((1, rows), F32),
            pltpu.VMEM((n_mom, 1, rows), F32),
            pltpu.VMEM((bands, 2, LANES, LANES), F32),
            pltpu.VMEM(((HALF + 1) * share, 2 * LANES), F32),
            dma((bands,)),
            dma((bands,)),
            dma((bands,)),
            dma((bands,)),
            dma((2,)),
            dma((2,)),
            dma((2,)),
            dma((2,)),
            dma((2,)),
            dma((8,)),
            regular((n_mom,)),
            regular,
        ],
        compiler_params=pltpu.CompilerParams(
            collective_id=0, has_side_effects=True, vmem_limit_bytes=52 * 1024 * 1024
        ),
    )(
        *(
            pltpu.with_memory_space_constraint(operand, pltpu.HBM)
            for operand in (
                quasi_probability_grid,
                potential_energy_map,
                contact_inflow_states,
                crystal_kelvin_field[None],
                area_index_map[None],
                damping_ratio_per_step[None],
                equilibrium_populace[None],
                conductance_per_step[None],
            )
        )
    )
    updated, warm = pl.pallas_call(
        write_out,
        out_shape=shapes,
        in_specs=[vmem, vmem],
        out_specs=(hbm, hbm),
        scratch_shapes=[dma((bands + 1,))],
        compiler_params=pltpu.CompilerParams(vmem_limit_bytes=8 * 1024 * 1024),
    )(updated, warm)
    return updated, warm[0]


def solution(mesh):
    return jax.shard_map(
        body,
        mesh=mesh,
        in_specs=(
            P(None, "pos", "mom"),
            P(None, "pos"),
            P(None, None, "mom"),
            P("pos"),
            P("pos"),
            P(),
            P(),
            P(),
        ),
        out_specs=(P(None, "pos", "mom"), P("pos")),
        check_vma=False,
    )
```

```python
import functools

import jax
import jax.numpy as jnp
import numpy as np
from jax import lax
from jax.experimental import pallas as pl
from jax.experimental.pallas import tpu as pltpu
from jax.sharding import PartitionSpec as P

K = 8192
LANES = 128
FOLD = K // LANES
HALF = FOLD // 2

courant = 0.9
energy_top = 3.0
energy_shift = 0.25
band_offset = 0.5
potential_gain = 0.5
heat_gain = 0.5
heat_outflow = 0.1

F32 = jnp.float32
BF16 = jnp.bfloat16
MESH = pl.DeviceIdType.MESH


def unit_root(step, length):
    angle = 2.0 * np.pi * step / length
    return float(np.cos(angle)), float(np.sin(angle))


def turned(re, im, c, s):
    if s == 0.0 and c == 1.0:
        return re, im
    if im is None:
        return re * c, re * s
    if abs(c) < 1e-12:
        return -im * s, re * s
    return re * c - im * s, re * s + im * c


def plus(a, b):
    if a is None:
        return b
    if b is None:
        return a
    return a + b


def minus(a, b):
    if b is None:
        return a
    if a is None:
        return -b
    return a - b


def real_forward(xs):
    n = len(xs)
    if n == 2:
        return [(xs[0] + xs[1], None), (xs[0] - xs[1], None)]
    even, odd = real_forward(xs[0::2]), real_forward(xs[1::2])
    out = [None] * (n // 2 + 1)
    for k in range(n // 4 + 1):
        c, s = unit_root(k, n)
        orr, oi = turned(odd[k][0], odd[k][1], c, s)
        er, ei = even[k]
        if 4 * k == n:
            out[k] = (er, odd[k][0])
            continue
        out[k] = (er + orr, plus(ei, oi))
        low = minus(oi, ei)
        out[n // 2 - k] = (er - orr, low)
    return out


def real_inverse(spec):
    n = 2 * (len(spec) - 1)
    if n == 2:
        a, b = spec[0][0], spec[1][0]
        return [a + b, a - b]
    even, odd = [], []
    for k in range(n // 4 + 1):
        ar, ai = spec[k]
        br, bi = spec[n // 2 - k]
        c, s = unit_root(k, n)
        if 4 * k == n:
            even.append((ar + ar, None))
            odd.append((-(ai + ai), None))
            continue
        if k == 0:
            even.append((ar + br, None))
            odd.append((ar - br, None))
            continue
        even.append((ar + br, minus(ai, bi)))
        odd.append(turned(ar - br, plus(ai, bi), c, s))
    xe, xo = real_inverse(even), real_inverse(odd)
    out = [None] * n
    out[0::2], out[1::2] = xe, xo
    return out


def fill_tables(weight_ref, twist_ref):
    row = lax.broadcasted_iota(jnp.int32, (LANES, LANES), 0)
    lane = lax.broadcasted_iota(jnp.int32, (LANES, LANES), 1)
    angle = lax.rem(row * lane, LANES).astype(F32) * (2.0 * np.pi / LANES)
    c, s = jnp.cos(angle), jnp.sin(angle)
    for n, blocks in enumerate((((c, s), (-s, c)), ((c, -s), (s, c)))):
        for a in range(2):
            for b in range(2):
                at = (pl.ds(a * LANES, LANES), pl.ds(b * LANES, LANES))
                high = blocks[a][b].astype(BF16)
                weight_ref[(2 * n,) + at] = high
                weight_ref[(2 * n + 1,) + at] = (blocks[a][b] - high.astype(F32)).astype(BF16)
    count = twist_ref.shape[1]
    angle = (row * lane)[:count].astype(F32) * (2.0 * np.pi / K)
    twist_ref[0] = jnp.cos(angle)
    twist_ref[1] = jnp.sin(angle)


def split_dot(a, high, low):
    a_high = a.astype(BF16)
    a_low = (a - a_high.astype(F32)).astype(BF16)
    dot = functools.partial(jnp.dot, preferred_element_type=F32)
    return dot(a_high, high) + (dot(a_low, high) + dot(a_high, low))


def kernel(
    sizes,
    grid_hbm,
    pot_hbm,
    contact_hbm,
    warmth_hbm,
    area_hbm,
    damping_hbm,
    populace_hbm,
    conduct_hbm,
    out_ref,
    warm_ref,
    grid_ref,
    pot_ref,
    contact_ref,
    warmth_ref,
    area_ref,
    damping_ref,
    populace_ref,
    conduct_ref,
    weight_ref,
    twist_ref,
    recv,
    back_send,
    back_recv,
    halo_low,
    halo_high,
    pot_all,
    warmth_all,
    heat_send,
    heat_all,
    pot_table,
    work,
    send_sem,
    fwd_recv_sem,
    ret_recv_sem,
    halo_send_sem,
    halo_recv_sem,
    small_send_sem,
    small_recv_sem,
    heat_sem,
    load_sem,
    mom_ready,
    pos_ready,
):
    bands, rows, cols, n_pos, n_mom = sizes
    share = rows // n_mom
    pieces = cols // LANES
    grid_len = n_pos * rows
    pos = lax.axis_index("pos")
    me = lax.axis_index("mom")

    mom_in = inner_size(n_mom)
    mom_out = n_mom // mom_in
    m_hi, m_lo = me // mom_in, lax.rem(me, mom_in)

    def pos_peer(d):
        return lax.rem(pos + d, n_pos)

    def over_peers(do):
        for d in range(1, n_mom):
            do(lax.rem(me + d, n_mom))

    def wait_all(ref, count, sem):
        block = ref.at[pl.ds(0, count)]
        pltpu.make_async_copy(block, block, sem).wait()

    small = (
        (pot_hbm, pot_ref),
        (contact_hbm, contact_ref),
        (warmth_hbm, warmth_ref),
        (area_hbm, area_ref),
        (damping_hbm, damping_ref),
        (populace_hbm, populace_ref),
        (conduct_hbm, conduct_ref),
    )
    loads = [
        pltpu.make_async_copy(src, dst, load_sem.at[n])
        for n, (src, dst) in enumerate(((grid_hbm, grid_ref),) + small)
    ]

    def small_copy(d, which):
        return pltpu.make_async_remote_copy(
            src_ref=warmth_hbm if which else pot_hbm,
            dst_ref=(warmth_all if which else pot_all).at[pos],
            send_sem=small_send_sem.at[which],
            recv_sem=small_recv_sem.at[which],
            device_id=(pos_peer(d), me),
            device_id_type=MESH,
        )

    def halo_copy(up):
        return pltpu.make_async_remote_copy(
            src_ref=grid_hbm.at[:, pl.ds(rows - 8, 8) if up else pl.ds(0, 8), :],
            dst_ref=halo_low if up else halo_high,
            send_sem=halo_send_sem.at[0 if up else 1],
            recv_sem=halo_recv_sem.at[0 if up else 1],
            device_id=(pos_peer(1 if up else n_pos - 1), me),
            device_id_type=MESH,
        )

    def forward_copy(band, peer):
        return pltpu.make_async_remote_copy(
            src_ref=grid_hbm.at[band, pl.ds(pl.multiple_of(peer * share, share), share), :],
            dst_ref=recv.at[band, me],
            send_sem=send_sem.at[0],
            recv_sem=fwd_recv_sem.at[band],
            device_id=(pos, peer),
            device_id_type=MESH,
        )

    def return_copy(band, peer):
        return pltpu.make_async_remote_copy(
            src_ref=back_send.at[band, peer],
            dst_ref=back_recv.at[band, me],
            send_sem=send_sem.at[1],
            recv_sem=ret_recv_sem.at[band],
            device_id=(pos, peer),
            device_id_type=MESH,
        )

    def heat_copy(peer):
        return pltpu.make_async_remote_copy(
            src_ref=heat_send,
            dst_ref=heat_all.at[me],
            send_sem=heat_sem.at[0],
            recv_sem=heat_sem.at[1],
            device_id=(pos, peer),
            device_id_type=MESH,
        )

    def start_forward(band, peer):
        forward_copy(band, peer).start()

    for load in loads:
        load.start()

    def under(peer):
        return (peer // mom_in <= m_hi) & (peer % mom_in <= m_lo) & (peer != me)

    def over(peer):
        return (peer // mom_in >= m_hi) & (peer % mom_in >= m_lo) & (peer != me)

    upper_row = mom_out // 2 if mom_out % 2 == 0 else mom_out
    at_middle = m_hi == upper_row - 1 if mom_out % 2 == 0 else m_hi < 0
    barrier = pltpu.get_barrier_semaphore()

    @pl.when(m_hi == upper_row)
    def _():
        pl.semaphore_signal(barrier, inc=1, device_id=(pos, me - mom_in), device_id_type=MESH)

    for peer in range(1, n_mom):

        @pl.when(over(peer))
        def _(peer=peer):
            pl.semaphore_signal(barrier, inc=1, device_id=(pos, peer), device_id_type=MESH)

    for peer in range(1, n_pos):

        @pl.when(pos < peer)
        def _(peer=peer):
            pl.semaphore_signal(barrier, inc=1, device_id=(peer, me), device_id_type=MESH)

    below = (m_hi + 1) * (m_lo + 1) - 1 + pos + jnp.where(at_middle, 1, 0)

    @pl.when(below > 0)
    def _():
        pl.semaphore_wait(barrier, below)

    @pl.when(at_middle)
    def _():
        start_forward(0, me + mom_in)

    for peer in range(n_mom - 1):
        pl.when(under(peer))(functools.partial(start_forward, 0, peer))

    for peer in reversed(range(n_mom - 1)):

        @pl.when(under(peer))
        def _(peer=peer):
            pl.semaphore_signal(
                mom_ready.at[me], inc=1, device_id=(pos, peer), device_id_type=MESH
            )


    for peer in range(n_pos - 1):

        @pl.when(peer < pos)
        def _(peer=peer):
            pl.semaphore_signal(pos_ready, inc=1, device_id=(peer, me), device_id_type=MESH)

    fill_tables(weight_ref, twist_ref)

    steps = [(i, j) for i in range(mom_out) for j in range(mom_in) if i or j]
    for d_hi, d_lo in sorted(steps, key=lambda step: (sum(step), -step[0])):
        top_hi, top_lo = m_hi + d_hi, m_lo + d_lo
        valid = (top_hi < mom_out) & (top_lo < mom_in)

        @pl.when(valid)
        def _(d_hi=d_hi, d_lo=d_lo, top_hi=top_hi, top_lo=top_lo):
            pl.semaphore_wait(mom_ready.at[top_hi * mom_in + top_lo], 1)
            if d_hi and d_lo:
                start_forward(0, top_hi * mom_in + top_lo)
            elif d_hi:
                for lo in range(mom_in):
                    done = at_middle & (lo == m_lo) if d_hi == 1 else lo < 0
                    pl.when((lo <= m_lo) & jnp.logical_not(done))(
                        functools.partial(start_forward, 0, top_hi * mom_in + lo)
                    )
            else:
                for hi in range(mom_out):
                    pl.when(hi <= m_hi)(
                        functools.partial(start_forward, 0, hi * mom_in + top_lo)
                    )

    @pl.when(pos < n_pos - 1)
    def _():
        pl.semaphore_wait(pos_ready, n_pos - 1 - pos)

    for d in range(1, n_pos):
        small_copy(d, 0).start()
        small_copy(d, 1).start()

    @pl.when(pos < n_pos - 1)
    def _():
        halo_copy(True).start()

    @pl.when(pos > 0)
    def _():
        halo_copy(False).start()

    for band in range(1, bands):
        over_peers(functools.partial(start_forward, band))
    for load in loads:
        load.wait()

    own = pl.ds(pl.multiple_of(me * share, share), share)
    for band in range(bands):
        recv[band, me] = grid_ref[band, own, :]
    pot_all[pos] = pot_ref[...]
    warmth_all[pos] = warmth_ref[...]

    @pl.when(pos == 0)
    def _():
        halo_low[:, 7:8, :] = contact_ref[:, 0:1, :]

    @pl.when(pos > 0)
    def _():
        halo_copy(True).wait_recv()

    @pl.when(pos == n_pos - 1)
    def _():
        halo_high[:, 0:1, :] = contact_ref[:, 1:2, :]

    @pl.when(pos < n_pos - 1)
    def _():
        halo_copy(False).wait_recv()

    def picked(values):
        total = jnp.zeros((1, rows), F32)
        for n in range(values.shape[1]):
            total = jnp.where(area_ref[...] == n, values[0:1, n : n + 1], total)
        return total

    def column(row):
        return jnp.transpose(jnp.broadcast_to(row, (rows, rows)))

    warmth = warmth_ref[...]
    relax = picked(damping_ref)
    conduct = picked(conduct_ref)
    warmth_col = column(warmth)
    relax_col = column(relax)
    dens_col = column(picked(populace_ref))
    cold_col = -1.0 / warmth_col
    row_iota = lax.broadcasted_iota(jnp.int32, (rows, LANES), 0)

    def local_piece(c, heat):
        lane = pl.ds(pl.multiple_of(c * LANES, LANES), LANES)
        mom = lax.broadcasted_iota(jnp.int32, (1, LANES), 1) + (me * cols + c * LANES)
        unit = (2.0 * mom.astype(F32) + 1.0) / K - 1.0
        velocity = courant * unit
        energy = energy_top * (unit + energy_shift) ** 2
        for band in range(bands):
            f = grid_ref[band, :, lane]
            below = jnp.where(row_iota == 0, halo_low[band, 7:8, lane], pltpu.roll(f, 1, 0))
            above = jnp.where(
                row_iota == rows - 1, halo_high[band, 0:1, lane], pltpu.roll(f, rows - 1, 0)
            )
            drift = -velocity * jnp.where(velocity > 0, f - below, above - f)
            excess = f - dens_col * jnp.exp((energy + band_offset * band) * cold_col)
            out_ref[band, :, lane] = f + drift - relax_col * excess
            heat = heat + energy * excess
        return heat

    heat = lax.fori_loop(0, pieces, local_piece, jnp.zeros((rows, LANES), F32))
    heat_row = jnp.sum(jnp.transpose(heat), axis=0, keepdims=True)
    heat_send[...] = heat_row
    heat_all[me] = heat_row
    over_peers(lambda peer: heat_copy(peer).start())

    wait_all(pot_all, n_pos - 1, small_recv_sem.at[0])
    wait_all(warmth_all, n_pos - 1, small_recv_sem.at[1])
    n_step = grid_len // FOLD
    base = pos * rows + me * share - HALF
    turn = lax.rem(2 * grid_len - base, grid_len)
    step_iota = lax.broadcasted_iota(jnp.int32, (n_step, grid_len), 0)
    place_iota = lax.broadcasted_iota(jnp.int32, (LANES, LANES), 0)
    lane_iota = lax.broadcasted_iota(jnp.int32, (LANES, LANES), 1)
    signed = jnp.where(lane_iota < LANES // 2, lane_iota, lane_iota - LANES) * FOLD
    for band in range(bands):
        profile = jnp.concatenate(
            [pot_all[j, band : band + 1, :] for j in range(n_pos)], axis=1
        )
        first = profile[:, 0:1]
        last = profile[:, grid_len - 1 : grid_len]
        profile = jnp.broadcast_to(profile, (n_step, grid_len))
        for side in range(2):
            stack = profile
            for m in range(1, n_step):
                shift = (grid_len - FOLD * m) % grid_len if side == 0 else FOLD * m
                stack = jnp.where(step_iota == m, pltpu.roll(profile, shift, 1), stack)
            stack = pltpu.roll(stack, turn, 1)[:, :LANES]
            stack = jnp.transpose(jnp.concatenate([stack] * (LANES // n_step), axis=0))
            index = base + place_iota + (signed if side == 0 else -signed)
            stack = jnp.where(index < 0, first, jnp.where(index > grid_len - 1, last, stack))
            pot_table[band, side] = stack

    scale = potential_gain / K

    def forward_wait(band):
        wait_all(recv.at[band], n_mom - 1, fwd_recv_sem.at[band])

    def transform(band):
        cells = [
            recv[band, j, :, c * LANES : (c + 1) * LANES]
            for j in range(n_mom)
            for c in range(pieces)
        ]
        spec = real_forward(cells)
        for s, (re, im) in enumerate(spec):
            at = pl.ds(s * share, share)
            c_row, s_row = twist_ref[0, s : s + 1, :], twist_ref[1, s : s + 1, :]
            if im is None:
                work[at, :LANES] = re * c_row
                work[at, LANES:] = re * s_row
            else:
                work[at, :LANES] = re * c_row - im * s_row
                work[at, LANES:] = re * s_row + im * c_row
        work[...] = split_dot(work[...], weight_ref[0], weight_ref[1])
        for s in range(HALF + 1):
            at = pl.ds(s * share, share)
            differ = (
                pot_table[band, 0, HALF + s : HALF + s + share, :]
                - pot_table[band, 1, HALF - s : HALF - s + share, :]
            ) * scale
            work[at, :LANES] = work[at, :LANES] * differ
            work[at, LANES:] = work[at, LANES:] * differ
        work[...] = split_dot(work[...], weight_ref[2], weight_ref[3])
        spec = []
        for s in range(HALF + 1):
            at = pl.ds(s * share, share)
            c_row, s_row = twist_ref[0, s : s + 1, :], twist_ref[1, s : s + 1, :]
            re, im = work[at, :LANES], work[at, LANES:]
            spec.append((im * c_row - re * s_row, re * c_row + im * s_row))
        cells = real_inverse(spec)
        for j in range(n_mom):
            for c in range(pieces):
                back_send[band, j, :, c * LANES : (c + 1) * LANES] = cells[j * pieces + c]
        back_recv[band, me] = back_send[band, me]

    def return_start(band):
        over_peers(lambda peer: return_copy(band, peer).start())

    def one_band(band, carry):
        forward_wait(band)

        transform(band)
        return_start(band)
        return carry

    lax.fori_loop(0, bands, one_band, 0)

    def add_back(band, carry):
        wait_all(back_recv.at[band], n_mom - 1, ret_recv_sem.at[band])
        for j in range(n_mom):
            at = pl.ds(j * share, share)
            out_ref[band, at, :] = out_ref[band, at, :] + back_recv[band, j]
        return carry

    lax.fori_loop(0, bands - 1, add_back, 0)

    wait_all(heat_all, n_mom - 1, heat_sem.at[1])
    total = heat_all[0]
    for j in range(1, n_mom):
        total = total + heat_all[j]
    lane_row = lax.broadcasted_iota(jnp.int32, (1, rows), 1)
    low_edge = warmth_all[jnp.maximum(pos - 1, 0), 0:1, rows - 1 : rows]
    high_edge = warmth_all[jnp.minimum(pos + 1, n_pos - 1), 0:1, 0:1]
    low_edge = jnp.where(pos == 0, jnp.ones_like(low_edge), low_edge)
    high_edge = jnp.where(pos == n_pos - 1, jnp.ones_like(high_edge), high_edge)
    before = jnp.where(lane_row == 0, low_edge, pltpu.roll(warmth, 1, 1))
    after = jnp.where(lane_row == rows - 1, high_edge, pltpu.roll(warmth, rows - 1, 1))
    warm_ref[...] = (
        warmth
        + conduct * (after - 2.0 * warmth + before)
        + heat_gain / K * relax * total
        - heat_outflow * (warmth - 1.0)
    )

    wait_all(pot_all, n_pos - 1, small_send_sem.at[0])
    wait_all(warmth_all, n_pos - 1, small_send_sem.at[1])

    @pl.when(pos < n_pos - 1)
    def _():
        halo_copy(True).wait_send()

    @pl.when(pos > 0)
    def _():
        halo_copy(False).wait_send()

    wait_all(heat_all, n_mom - 1, heat_sem.at[0])
    sent = recv.at[:, pl.ds(0, n_mom - 1)]
    pltpu.make_async_copy(sent, sent, send_sem.at[0]).wait()
    add_back(bands - 1, 0)
    sent = back_send.at[:, pl.ds(0, n_mom - 1)]
    pltpu.make_async_copy(sent, sent, send_sem.at[1]).wait()


def write_out(grid_ref, warm_ref, grid_hbm, warm_hbm, sem):
    bands = grid_ref.shape[0]
    copies = [
        pltpu.make_async_copy(grid_ref.at[band], grid_hbm.at[band], sem.at[band])
        for band in range(bands)
    ]
    copies.append(pltpu.make_async_copy(warm_ref, warm_hbm, sem.at[bands]))
    for copy in copies:
        copy.start()
    for copy in copies:
        copy.wait()


def inner_size(n):
    inner = 1
    while inner * inner * 4 <= n:
        inner *= 2
    return inner if n % inner == 0 else 1


def body(
    quasi_probability_grid,
    potential_energy_map,
    contact_inflow_states,
    crystal_kelvin_field,
    area_index_map,
    damping_ratio_per_step,
    equilibrium_populace,
    conductance_per_step,
):
    bands, rows, cols = quasi_probability_grid.shape
    n_pos = lax.axis_size("pos")
    n_mom = lax.axis_size("mom")
    share = rows // n_mom
    kinds = damping_ratio_per_step.shape[0]
    vmem = pl.BlockSpec(memory_space=pltpu.VMEM)
    hbm = pl.BlockSpec(memory_space=pltpu.HBM)
    dma = pltpu.SemaphoreType.DMA
    regular = pltpu.SemaphoreType.REGULAR
    shapes = (
        jax.ShapeDtypeStruct((bands, rows, cols), F32),
        jax.ShapeDtypeStruct((1, rows), F32),
    )
    updated, warm = pl.pallas_call(
        functools.partial(kernel, (bands, rows, cols, n_pos, n_mom)),
        out_shape=shapes,
        in_specs=[hbm] * 8,
        out_specs=(vmem, vmem),
        scratch_shapes=[
            pltpu.VMEM((bands, rows, cols), F32),
            pltpu.VMEM((bands, rows), F32),
            pltpu.VMEM((bands, 2, cols), F32),
            pltpu.VMEM((1, rows), F32),
            pltpu.VMEM((1, rows), jnp.int32),
            pltpu.VMEM((1, kinds), F32),
            pltpu.VMEM((1, kinds), F32),
            pltpu.VMEM((1, kinds), F32),
            pltpu.VMEM((4, 2 * LANES, 2 * LANES), BF16),
            pltpu.VMEM((2, HALF + 8, LANES), F32),
            pltpu.VMEM((bands, n_mom, share, cols), F32),
            pltpu.VMEM((bands, n_mom, share, cols), F32),
            pltpu.VMEM((bands, n_mom, share, cols), F32),
            pltpu.VMEM((bands, 8, cols), F32),
            pltpu.VMEM((bands, 8, cols), F32),
            pltpu.VMEM((n_pos, bands, rows), F32),
            pltpu.VMEM((n_pos, 1, rows), F32),
            pltpu.VMEM((1, rows), F32),
            pltpu.VMEM((n_mom, 1, rows), F32),
            pltpu.VMEM((bands, 2, LANES, LANES), F32),
            pltpu.VMEM(((HALF + 1) * share, 2 * LANES), F32),
            dma((2,)),
            dma((bands,)),
            dma((bands,)),
            dma((2,)),
            dma((2,)),
            dma((2,)),
            dma((2,)),
            dma((2,)),
            dma((8,)),
            regular((n_mom,)),
            regular,
        ],
        compiler_params=pltpu.CompilerParams(
            collective_id=0, has_side_effects=True, vmem_limit_bytes=52 * 1024 * 1024
        ),
    )(
        *(
            pltpu.with_memory_space_constraint(operand, pltpu.HBM)
            for operand in (
                quasi_probability_grid,
                potential_energy_map,
                contact_inflow_states,
                crystal_kelvin_field[None],
                area_index_map[None],
                damping_ratio_per_step[None],
                equilibrium_populace[None],
                conductance_per_step[None],
            )
        )
    )
    updated, warm = pl.pallas_call(
        write_out,
        out_shape=shapes,
        in_specs=[vmem, vmem],
        out_specs=(hbm, hbm),
        scratch_shapes=[dma((bands + 1,))],
        compiler_params=pltpu.CompilerParams(vmem_limit_bytes=8 * 1024 * 1024),
    )(updated, warm)
    return updated, warm[0]


def solution(mesh):
    return jax.shard_map(
        body,
        mesh=mesh,
        in_specs=(
            P(None, "pos", "mom"),
            P(None, "pos"),
            P(None, None, "mom"),
            P("pos"),
            P("pos"),
            P(),
            P(),
            P(),
        ),
        out_specs=(P(None, "pos", "mom"), P("pos")),
        check_vma=False,
    )
```
